32 devices in a mesh: wide: 16 (over z, y, core), narrow: 2 (over x).
Axes of the slice: x: 2, y: 2, z: 4, core: 2. Of those that a mesh axis runs over, the one named last changes fastest.
Arguments:
- amplitudes: bfloat16 [65536, 1024], P(('wide', 'narrow')), may hold values from -0.046875 to 0.046875
- integral_slab: bfloat16 [65536, 1024], P(('wide', 'narrow')), may hold values from -0.046875 to 0.046875
- coupling: float32 [32, 1024, 1024], P(('wide', 'narrow')), may hold values from -0.046875 to 0.046875
- pair_of_block: int32 [32], replicated, may hold values from 0 to 31, each once
- pair_shift: float32 [32], replicated, may hold values from -4 to 4
- virt_energy: float32 [1024], replicated, may hold values from 0 to 26
- core_energy: float32 [64], replicated, may hold values from -6 to -4
- core_index: int32 [2], replicated, may hold values from 0 to 63, as said below
- frequency: float32 [16], replicated, may hold values from 6 to 30
- dipole: float32 [64, 1024], P(None, 'narrow'), may hold values from -6 to 6
Outputs:
- response: float32 [2, 32, 1024], P(None, None, 'narrow')
- residual_rms: float32 [2, 32], replicated
The draws below stay inside these ranges and needn't reach their ends.
Inputs may be any that keep to these rules, and one draw needn't show every extreme that they name: `core_index`: the 2 core orbitals are different occupied orbitals, and the last of them is orbital 64 - 1.
All inputs are finite; a program needn't handle non-finite values.
Results may differ from the reference program's by a relative error of at most 0.0003.
Values sent between devices are 32-bit elements; how exact they have to be, the bound alone decides.
No kernel may reach another device: no remote copies, remote signals or barrier semaphores. Data moves between devices by JAX's collectives and lax.ppermute only.
A program may use at most 64 MiB of HBM per device.

```python
import jax
import jax.numpy as jnp
from jax import lax

NV = 1024
NOCC = 64
NF = 16
NCORE = 2
ITERS = 2
ROWS_DEV = 2048
ROWS = 65536
PAIRS = 32
CF = 32
DEVICES = 32


def draw_core_index(key, part):
    order = jax.random.permutation(jax.random.fold_in(key, 7), NOCC - 1)
    others = order[:NCORE - 1].astype(jnp.int32)
    return jnp.concatenate([others, jnp.full((1,), NOCC - 1, jnp.int32)], 0)


def draw_frequency(key, part):
    subkey = jax.random.fold_in(key, 11)
    places = jnp.arange(NF, dtype=jnp.float32)
    jitter = jnp.clip(0.5 + 0.12 * jax.random.normal(subkey, (NF,), jnp.float32), 0.2, 0.8)
    return (6.0 + 24.0 * (places + jitter) / NF).astype(jnp.float32)


def strengthened(drawn, own_key, source, target, parts, factor):
    def block_of(position):
        return (jnp.arange(drawn.shape[position]) // (drawn.shape[position] // parts)).reshape((-1,) + (1,) * (drawn.ndim - 1 - position))

    first = jax.random.permutation(own_key, parts)[block_of(target)]
    other_side = (block_of(target) + parts // 2) % parts
    return jnp.where((block_of(source) == first) | (block_of(source) == other_side), factor * drawn, drawn)


def level_of(key, dims, pieces, least, high):
    factor_of, own = 1.0, jax.random.fold_in(key, 6)
    for axis_at, parts in pieces:
        heights = jnp.exp(jax.random.uniform(jax.random.fold_in(own, axis_at), (parts,), jnp.float32, least / len(pieces), high / len(pieces)))
        factor_of = factor_of * jnp.repeat(heights, dims[axis_at] // parts).reshape([-1 if axis == axis_at else 1 for axis in range(len(dims))])
    return factor_of


def noise(rng, shape, width, most, shards=(), kind=jnp.bfloat16):
    drawn = width * jax.random.normal(rng, shape, jnp.float32)
    if shards:
        drawn = drawn * level_of(rng, shape, shards, -0.22, 0.18)
    return jnp.clip(drawn, -most, most).astype(kind)


def bell_draw_with(rng, extent, spread, reach, pieces, heavy, kind=jnp.bfloat16):
    entries = spread * jax.random.normal(rng, extent, jnp.float32)
    if pieces:
        entries = entries * level_of(rng, extent, pieces, -0.22, 0.18)
    return jnp.clip(strengthened(entries, jax.random.fold_in(rng, 3), *heavy), -reach, reach).astype(kind)


def setup_inputs(seed: int = 0) -> dict:
    key_of = jax.random.split(jax.random.key(seed), 11)
    amplitudes = bell_draw_with(key_of[0], (ROWS, NV), ROWS ** -0.5, 0.046875, ((0, 32),), (0, 1, 32, 2.75))
    integral_slab = noise(key_of[1], (ROWS, NV), (16 * NV) ** -0.5, 0.046875, ((0, 32),))
    coupling = noise(key_of[2], (PAIRS, NV, NV), (16 * NV) ** -0.5, 0.046875, ((0, 32),), jnp.float32)
    pair_of_block = jax.random.permutation(key_of[3], PAIRS).astype(jnp.int32)
    pair_shift = jnp.clip(jax.random.uniform(key_of[4], (PAIRS,), jnp.float32, -4.0, 4.0), -4.0, 4.0)
    virt_energy = jnp.clip(jax.random.uniform(key_of[5], (NV,), jnp.float32, 0.0, 26.0), 0.0, 26.0)
    core_energy = jnp.clip(jax.random.uniform(key_of[6], (NOCC,), jnp.float32, -6.0, -4.0), -6.0, -4.0)
    core_index = draw_core_index(jax.random.fold_in(key_of[10], 71), 0)
    frequency = draw_frequency(jax.random.fold_in(key_of[10], 71), 0)
    dipole = noise(key_of[9], (NOCC, NV), 1.0, 6.0, ((1, 2),), jnp.float32)
    return {"amplitudes": amplitudes, "integral_slab": integral_slab, "coupling": coupling, "pair_of_block": pair_of_block, "pair_shift": pair_shift, "virt_energy": virt_energy, "core_energy": core_energy, "core_index": core_index, "frequency": frequency, "dipole": dipole}


damping = 0.5
highest = lax.Precision.HIGHEST

def divide_precond(real_part, imag_part, level, level_mag):
    return ((real_part * level - imag_part * damping) / level_mag, (imag_part * level + real_part * damping) / level_mag)

def divide_denom(real_part, imag_part, denom_real, denom_mag):
    return ((real_part * denom_real + imag_part * damping) / denom_mag, (imag_part * denom_real - real_part * damping) / denom_mag)

def apply_precond(real_part, imag_part, level):
    return (level * real_part + damping * imag_part, level * imag_part - damping * real_part)

def reference(amplitudes, integral_slab, coupling, pair_of_block, pair_shift, virt_energy, core_energy, core_index, frequency, dipole):
    row_blocks = amplitudes.reshape(DEVICES, ROWS_DEV, NV)
    slab_blocks = integral_slab.reshape(DEVICES, ROWS_DEV, NV)

    def accumulate(total, blocks):
        left_block, right_block = blocks
        product = lax.dot_general(left_block, right_block, (((0,), (0,)), ((), ())), preferred_element_type=jnp.float32)
        return (total + product, None)
    singles, _ = lax.scan(accumulate, jnp.zeros((NV, NV), jnp.float32), (row_blocks, slab_blocks))
    picked_energy = core_energy[core_index]
    shift = (frequency[None, :] + picked_energy[:, None]).reshape(-1)
    level = virt_energy[None, :] - shift[:, None]
    level_mag = level * level + damping * damping
    rhs = jnp.repeat(dipole[core_index], NF, axis=0)
    resp_re, resp_im = divide_precond(rhs, jnp.zeros_like(rhs), level, level_mag)
    slot_shift = pair_shift[pair_of_block]

    def fold_pairs(flattened):

        def one_slot(total, slot_data):
            matrix, offset = slot_data
            doubles_in = jnp.dot(flattened, matrix.T, precision=highest)
            denom_real = shift[:, None] - offset - virt_energy[None, :]
            denom_mag = denom_real * denom_real + damping * damping
            out_re, out_im = divide_denom(doubles_in[:CF], doubles_in[CF:], denom_real, denom_mag)
            outgoing = jnp.concatenate([out_re, out_im], 0)
            return (total + jnp.dot(outgoing, matrix, precision=highest), None)
        folded, _ = lax.scan(one_slot, jnp.zeros_like(flattened), (coupling, slot_shift))
        return folded
    rms_rows = []
    for sweep in range(ITERS):
        flattened = jnp.concatenate([resp_re, resp_im], 0)
        folded = fold_pairs(flattened)
        singles_term = jnp.dot(flattened, singles.T, precision=highest)
        applied = singles_term + folded
        app_re, app_im = apply_precond(resp_re, resp_im, level)
        res_re = rhs - (app_re + applied[:CF])
        res_im = -(app_im + applied[CF:])
        squares = lax.optimization_barrier(jnp.sum(res_re * res_re + res_im * res_im, axis=1))
        rms_rows.append(jnp.sqrt(squares / (2 * NV) + 1e-06))
        step_re, step_im = divide_precond(res_re, res_im, level, level_mag)
        resp_re = resp_re + step_re
        resp_im = resp_im + step_im
    return (jnp.stack([resp_re, resp_im], 0), jnp.stack(rms_rows, 0))
```

```python
import jax
import jax.numpy as jnp
from jax import lax
from jax.sharding import PartitionSpec as P

ITERS = 2
DAMP = 0.5
HIGHEST = lax.Precision.HIGHEST
ROWS = (((0,), (0,)), ((), ()))
LAST = (((1,), (1,)), ((), ()))


def per_device(
    wide,
    narrow,
    amplitudes,
    integral_slab,
    coupling,
    pair_of_block,
    pair_shift,
    virt_energy,
    core_energy,
    core_index,
    frequency,
    dipole,
):
    virt = virt_energy.shape[0]
    freqs = frequency.shape[0]
    modes = freqs * core_index.shape[0]
    slots = coupling.shape[0]
    block = dipole.shape[1]
    everyone = modes % (wide * narrow) == 0
    group = ("wide", "narrow") if everyone else "wide"
    members = wide * narrow if everyone else wide
    owned = modes // members

    here = lax.axis_index(("wide", "narrow"))
    mine = lax.axis_index(group)
    picked = jnp.take(dipole, core_index, axis=0)
    picked = lax.all_gather(picked, "narrow", axis=1, tiled=True)
    shift = (frequency[None, :] + jnp.take(core_energy, core_index)[:, None]).reshape(-1)
    offset = jnp.take(pair_shift, lax.dynamic_slice_in_dim(pair_of_block, here * slots, slots))
    rhs = jnp.repeat(picked, freqs, axis=0)
    level = virt_energy[None, :] - shift[:, None]
    mag = level * level + DAMP * DAMP
    response = jnp.concatenate([rhs * level / mag, rhs * DAMP / mag], 0)
    den = shift[None, :, None] - offset[:, None, None] - virt_energy[None, None, :]
    den_mag = den * den + DAMP * DAMP
    own_rhs = lax.dynamic_slice_in_dim(rhs, mine * owned, owned)
    own_level = lax.dynamic_slice_in_dim(level, mine * owned, owned)
    own_mag = own_level * own_level + DAMP * DAMP
    own_re, own_im = own_rhs * own_level / own_mag, own_rhs * DAMP / own_mag
    slab = integral_slab.astype(jnp.float32)
    ampl = amplitudes.astype(jnp.float32)

    def dot(left, right, dims):
        return lax.dot_general(left, right, dims, precision=HIGHEST, preferred_element_type=jnp.float32)

    rms = []
    for sweep in range(ITERS):
        folded = dot(dot(response, slab, LAST), ampl, (((1,), (0,)), ((), ())))
        for slot in range(slots):
            inner = dot(response, coupling[slot], LAST)
            re, im = inner[:modes], inner[modes:]
            quot = jnp.concatenate(
                [
                    (re * den[slot] + im * DAMP) / den_mag[slot],
                    (im * den[slot] - re * DAMP) / den_mag[slot],
                ],
                0,
            )
            folded = folded + dot(quot, coupling[slot], (((1,), (0,)), ((), ())))
        pieces = folded.reshape(2, members, owned, virt).transpose(1, 0, 2, 3)
        total = jnp.sum(lax.all_to_all(pieces, group, 0, 0, tiled=True), 0)
        if not everyone:
            total = lax.psum(total, "narrow")
        res_re = own_rhs - (own_level * own_re + DAMP * own_im + total[0])
        res_im = -(own_level * own_im - DAMP * own_re + total[1])
        squares = jnp.sum(res_re * res_re + res_im * res_im, axis=1)
        rms.append(jnp.sqrt(squares / (2 * virt) + 1e-6))
        own_re = own_re + (res_re * own_level - res_im * DAMP) / own_mag
        own_im = own_im + (res_im * own_level + res_re * DAMP) / own_mag
        own = jnp.stack([own_re, own_im], 0)
        if sweep + 1 < ITERS:
            sent = jnp.broadcast_to(own[None], (members,) + own.shape)
            got = lax.all_to_all(sent, group, 0, 0, tiled=True)
            response = got.transpose(1, 0, 2, 3).reshape(2 * modes, virt)
    if everyone:
        sent = own.reshape(2, owned, narrow, block).transpose(2, 0, 1, 3)
        sent = jnp.broadcast_to(sent[None], (wide,) + sent.shape).reshape(members, 2, owned, block)
    else:
        sent = lax.dynamic_slice_in_dim(own, lax.axis_index("narrow") * block, block, 2)
        sent = jnp.broadcast_to(sent[None], (members,) + sent.shape)
    extra = jnp.broadcast_to(jnp.stack(rms, 0)[None, :, :, None], (members, 2, owned, 128))
    got = lax.all_to_all(jnp.concatenate([sent, extra], 3), group, 0, 0, tiled=True)
    got = got.transpose(1, 0, 2, 3).reshape(2, modes, block + 128)
    return got[:, :, :block], got[:, :, block]


def solution(mesh):
    wide, narrow = mesh.shape["wide"], mesh.shape["narrow"]
    split = ("wide", "narrow")

    def body(*args):
        return per_device(wide, narrow, *args)

    return jax.shard_map(
        body,
        mesh=mesh,
        in_specs=(
            P(split, None),
            P(split, None),
            P(split, None, None),
            P(),
            P(),
            P(),
            P(),
            P(),
            P(),
            P(None, "narrow"),
        ),
        out_specs=(P(None, None, "narrow"), P()),
        check_vma=False,
    )
```

```python
from functools import partial

import jax
import jax.numpy as jnp
from jax import lax
from jax.experimental import pallas as pl
from jax.experimental.pallas import tpu as pltpu
from jax.sharding import Mesh, PartitionSpec as P

ITERS = 2
DAMP = 0.5
HIGHEST = lax.Precision.HIGHEST
F32, BF16 = jnp.float32, jnp.bfloat16
LAST = (((1,), (1,)), ((), ()))
INNER = (((1,), (0,)), ((), ()))
SUB, LANE = 8, 128
VMEM = pl.BlockSpec(memory_space=pltpu.VMEM)
SMEM = pl.BlockSpec(memory_space=pltpu.SMEM)
HBM = pl.BlockSpec(memory_space=pl.ANY)


def mxu(left, right, dims):
    return lax.dot_general(left, right, dims, preferred_element_type=F32)


def halves(value):
    high = value.astype(BF16)
    return high, (value - high.astype(F32)).astype(BF16)


def stacked(value):
    return jnp.concatenate(halves(value), 0)


def joined(value):
    rows = value.shape[0] // 2
    return value[:rows] + value[rows:]


def call(body, name, operands, in_specs, outs, scratch=(), flops=0, moved=0):
    return pl.pallas_call(
        body,
        out_shape=[jax.ShapeDtypeStruct(s, d) for s, d in outs],
        in_specs=in_specs,
        out_specs=[VMEM] * len(outs),
        scratch_shapes=scratch,
        name=name,
        compiler_params=pltpu.CompilerParams(vmem_limit_bytes=20 << 20),
        cost_estimate=pl.CostEstimate(flops=flops, bytes_accessed=moved, transcendentals=0),
    )(*operands)


def pick_body(index, dipole, picked, sem):
    copies = [
        pltpu.make_async_copy(dipole.at[pl.ds(index[c], 1)], picked.at[pl.ds(c, 1)], sem.at[c])
        for c in range(index.shape[0])
    ]
    for copy in copies:
        copy.start()
    for copy in copies:
        copy.wait()


def prepare_body(
    index, energy, frequency, blocks, pair_shift, virt, coupling, level, denom, high, low
):
    freqs = frequency.shape[0]
    modes, columns = level.shape
    slots = coupling.shape[0]
    device = lax.axis_index(("chip", "core", "narrow"))
    rows = lax.broadcasted_iota(jnp.int32, (SUB, LANE), 0)
    tiles = []
    for start in range(0, modes, SUB):
        tile = jnp.zeros((SUB, LANE), F32)
        for k in range(start, start + SUB):
            value = frequency[k % freqs] + energy[index[k // freqs]]
            tile = jnp.where(rows == k - start, value, tile)
        tiles.append(tile)
    shift = jnp.concatenate(tiles, 0)
    for at in range(0, columns, LANE):
        here = jnp.broadcast_to(virt[:, at : at + LANE], (modes, LANE))
        level[:, at : at + LANE] = here - shift
        for s in range(slots):
            offset = pair_shift[blocks[device * slots + s]]
            denom[s, :, at : at + LANE] = (shift - offset) - here
    for s in range(slots):
        upper, lower = halves(coupling[s])
        high[s] = upper
        low[s] = lower


def fold(response, slab, denom, high, low):
    modes = response.shape[0] // 2
    upper, lower = halves(response)
    both = jnp.concatenate([upper, lower], 0)
    singles = stacked(joined(mxu(both, slab[...], LAST)))
    doubles = []
    for s in range(high.shape[0]):
        inner = joined(mxu(both, high[s], LAST)) + mxu(upper, low[s], LAST)
        re, im = inner[:modes], inner[modes:]
        den = denom[s]
        inverse = 1.0 / (den * den + DAMP * DAMP)
        doubles.append(
            stacked(
                jnp.concatenate(
                    [(re * den + im * DAMP) * inverse, (im * den - re * DAMP) * inverse], 0
                )
            )
        )
    return singles, doubles


def unfold(singles, doubles, amplitudes, high, low, columns):
    total = mxu(singles, amplitudes[:, columns], INNER)
    for s, outgoing in enumerate(doubles):
        total = total + mxu(outgoing, high[s, :, columns], INNER)
    total = joined(total)
    for s, outgoing in enumerate(doubles):
        total = total + mxu(outgoing[: outgoing.shape[0] // 2], low[s, :, columns], INNER)
    return total


def first_body(
    own, other, level, denom, high, low, slab, amplitudes, rhs, start, give, keep
):
    modes, virt = level.shape
    cores, block = own.shape
    freqs = modes // cores
    side = lax.axis_index("narrow")
    for part, at in ((own, side), (other, 1 - side)):
        columns = pl.ds(pl.multiple_of(at * block, LANE), block)
        for c in range(cores):
            rhs[c * freqs : (c + 1) * freqs, columns] = jnp.broadcast_to(
                part[c : c + 1], (freqs, block)
            )
    lev = level[...]
    inverse = 1.0 / (lev * lev + DAMP * DAMP)
    start[:modes] = rhs[...] * lev * inverse
    start[modes:] = rhs[...] * DAMP * inverse
    singles, doubles = fold(start[...], slab, denom, high, low)
    core = lax.axis_index("core")
    half = virt // 2
    for out, at in ((give, 1 - core), (keep, core)):
        columns = pl.ds(pl.multiple_of(at * half, LANE), half)
        total = unfold(singles, doubles, amplitudes, high, low, columns)
        for group in range(modes // SUB):
            for tile in range(half // LANE):
                piece = group * (half // LANE) + tile
                lanes = slice(tile * LANE, (tile + 1) * LANE)
                out[piece, 0] = total[group * SUB : (group + 1) * SUB, lanes]
                out[piece, 1] = total[modes + group * SUB : modes + (group + 1) * SUB, lanes]


def add_body(left, right, out):
    out[...] = left[...] + right[...]


def first_update_body(got, level, rhs, start, sent):
    members = got.shape[0]
    modes, virt = level.shape
    tiles = virt // 2 // LANE
    mine = lax.axis_index(("chip", "narrow"))
    group, tile = lax.div(mine, tiles), lax.rem(mine, tiles)
    column = lax.axis_index("core") * (virt // 2) + tile * LANE
    columns = pl.ds(pl.multiple_of(column, LANE), LANE)
    rows = pl.ds(pl.multiple_of(group * SUB, SUB), SUB)
    total = got[0]
    for j in range(1, members):
        total = total + got[j]
    lev, right = level[rows, columns], rhs[rows, columns]
    re = start[rows, columns]
    im = start[pl.ds(pl.multiple_of(modes + group * SUB, SUB), SUB), columns]
    inverse = 1.0 / (lev * lev + DAMP * DAMP)
    res_re = right - (lev * re + DAMP * im + total[0])
    res_im = -(lev * im - DAMP * re + total[1])
    re = re + (res_re * lev - res_im * DAMP) * inverse
    im = im + (res_im * lev + res_re * DAMP) * inverse
    for j in range(members):
        sent[j, 0] = re
        sent[j, 1] = im


def second_body(
    own, other, level, denom, high, low, slab, amplitudes, response, give, keep
):
    modes, virt = level.shape
    members = own.shape[0]
    half, quarter = virt // 2, virt // 4
    core = lax.axis_index("core")
    for part, at in ((own, core), (other, 1 - core)):
        for group in range(modes // SUB):
            for tile in range(half // LANE):
                piece = group * (half // LANE) + tile
                columns = pl.ds(pl.multiple_of(at * half + tile * LANE, LANE), LANE)
                response[group * SUB : (group + 1) * SUB, columns] = part[piece, 0]
                response[modes + group * SUB : modes + (group + 1) * SUB, columns] = part[piece, 1]
    singles, doubles = fold(response[...], slab, denom, high, low)
    owned = modes // members
    for out, at in ((give, 1 - core), (keep, core)):
        for side in range(2):
            columns = pl.ds(pl.multiple_of(side * half + at * quarter, LANE), quarter)
            total = unfold(singles, doubles, amplitudes, high, low, columns)
            lanes = slice(side * quarter, (side + 1) * quarter)
            for j in range(members):
                out[j, :owned, lanes] = total[j * owned : (j + 1) * owned]
                out[j, owned:, lanes] = total[modes + j * owned : modes + (j + 1) * owned]


def second_update_body(got, level, rhs, start, response, sent):
    members, double, width = got.shape
    owned = double // 2
    modes, virt = level.shape
    half, quarter = virt // 2, virt // 4
    mine = lax.axis_index(("chip", "narrow"))
    core = lax.axis_index("core")
    total = got[0]
    for j in range(1, members):
        total = total + got[j]
    per_tile = SUB // owned
    within = lax.rem(mine, per_tile)

    def own_rows(ref, first, columns):
        at = first + lax.div(mine, per_tile) * SUB
        tile = ref[pl.ds(pl.multiple_of(at, SUB), SUB), columns]
        rows = tile[:owned]
        for q in range(1, per_tile):
            rows = jnp.where(within == q, tile[q * owned : (q + 1) * owned], rows)
        return rows

    old_squares = jnp.zeros((owned, 1), F32)
    new_squares = jnp.zeros((owned, 1), F32)
    fresh = []
    for side in range(2):
        columns = pl.ds(pl.multiple_of(side * half + core * quarter, LANE), quarter)
        lanes = slice(side * quarter, (side + 1) * quarter)
        lev, right = own_rows(level, 0, columns), own_rows(rhs, 0, columns)
        re, im = own_rows(response, 0, columns), own_rows(response, modes, columns)
        step_re = re - own_rows(start, 0, columns)
        step_im = im - own_rows(start, modes, columns)
        old_re = lev * step_re + DAMP * step_im
        old_im = lev * step_im - DAMP * step_re
        old_squares += jnp.sum(old_re * old_re + old_im * old_im, axis=1, keepdims=True)
        inverse = 1.0 / (lev * lev + DAMP * DAMP)
        res_re = right - (lev * re + DAMP * im + total[:owned, lanes])
        res_im = -(lev * im - DAMP * re + total[owned:, lanes])
        new_squares += jnp.sum(res_re * res_re + res_im * res_im, axis=1, keepdims=True)
        re = re + (res_re * lev - res_im * DAMP) * inverse
        im = im + (res_im * lev + res_re * DAMP) * inverse
        fresh.append((re, im))
    squares = jnp.concatenate([old_squares, new_squares], 0)
    for j in range(members):
        re, im = fresh[j % 2]
        sent[j, :owned, :quarter] = re
        sent[j, owned:, :quarter] = im
        sent[j, :, quarter:] = jnp.broadcast_to(squares, (double, LANE))


def finish_body(own, other, response, rms):
    members, double, _ = own.shape
    owned = double // 2
    quarter = response.shape[2] // 2
    sweeps, modes = rms.shape
    core = lax.axis_index("core")
    for part, at in ((own, core), (other, 1 - core)):
        columns = pl.ds(pl.multiple_of(at * quarter, LANE), quarter)
        for j in range(members):
            for q in range(2):
                response[q, j * owned : (j + 1) * owned, columns] = part[
                    j, q * owned : (q + 1) * owned, :quarter
                ]
    row = lax.broadcasted_iota(jnp.int32, (sweeps, LANE), 0)
    lane = lax.broadcasted_iota(jnp.int32, (sweeps, LANE), 1)
    squares = jnp.zeros((sweeps, LANE), F32)
    for j in range(members):
        both = own[j, :, quarter:] + other[j, :, quarter:]
        for s in range(sweeps):
            for i in range(owned):
                at = s * owned + i
                value = jnp.broadcast_to(both[at : at + 1], (sweeps, LANE))
                squares = jnp.where((row == s) & (lane == j * owned + i), value, squares)
    virt = 4 * quarter
    rms[...] = jnp.sqrt(squares / (2 * virt) + 1e-6)[:, :modes]


def fast_path(
    chips,
    narrow,
    amplitudes,
    integral_slab,
    coupling,
    pair_of_block,
    pair_shift,
    virt_energy,
    core_energy,
    core_index,
    frequency,
    dipole,
):
    virt = virt_energy.shape[0]
    cores = core_index.shape[0]
    modes = frequency.shape[0] * cores
    slots = coupling.shape[0]
    block = dipole.shape[1]
    rows = amplitudes.shape[0]
    members = chips * narrow
    half = virt // 2
    flip_core = [(0, 1), (1, 0)]
    group = ("chip", "narrow")
    cost = dict(flops=8 * modes * virt * (virt * slots + rows), moved=4 * virt * (virt * slots + rows))

    (picked,) = call(
        pick_body,
        "pick",
        (core_index, dipole),
        [SMEM, HBM],
        [((cores, block), F32)],
        scratch=[pltpu.SemaphoreType.DMA((cores,))],
        moved=cores * block * 4,
    )
    across = lax.ppermute(picked, "narrow", flip_core)
    level, denom, high, low = call(
        prepare_body,
        "prepare",
        (core_index, core_energy, frequency, pair_of_block, pair_shift, virt_energy[None], coupling),
        [SMEM] * 5 + [VMEM] * 2,
        [
            ((modes, virt), F32),
            ((slots, modes, virt), F32),
            ((slots, virt, virt), BF16),
            ((slots, virt, virt), BF16),
        ],
        flops=4 * slots * virt * virt,
        moved=8 * slots * virt * virt,
    )
    piece = (members, 2, SUB, LANE)
    rhs, start, give, keep = call(
        first_body,
        "first",
        (picked, across, level, denom, high, low, integral_slab, amplitudes),
        [VMEM] * 8,
        [((modes, virt), F32), ((2 * modes, virt), F32), (piece, F32), (piece, F32)],
        **cost,
    )
    got = lax.ppermute(give, "core", flip_core)
    (total,) = call(add_body, "add_first", (keep, got), [VMEM] * 2, [(piece, F32)])
    got = lax.all_to_all(total, group, 0, 0, tiled=True)
    (sent,) = call(
        first_update_body, "first_update", (got, level, rhs, start), [VMEM] * 4, [(piece, F32)]
    )
    got = lax.all_to_all(sent, group, 0, 0, tiled=True)
    other = lax.ppermute(got, "core", flip_core)
    owned = modes // members
    piece = (members, 2 * owned, half)
    response, give, keep = call(
        second_body,
        "second",
        (got, other, level, denom, high, low, integral_slab, amplitudes),
        [VMEM] * 8,
        [((2 * modes, virt), F32), (piece, F32), (piece, F32)],
        **cost,
    )
    got = lax.ppermute(give, "core", flip_core)
    (total,) = call(add_body, "add_second", (keep, got), [VMEM] * 2, [(piece, F32)])
    got = lax.all_to_all(total, group, 0, 0, tiled=True)
    piece = (members, 2 * owned, half // 2 + LANE)
    (sent,) = call(
        second_update_body,
        "second_update",
        (got, level, rhs, start, response),
        [VMEM] * 5,
        [(piece, F32)],
    )
    got = lax.all_to_all(sent, group, 0, 0, tiled=True)
    other = lax.ppermute(got, "core", flip_core)
    return tuple(
        call(
            finish_body,
            "finish",
            (got, other),
            [VMEM] * 2,
            [((2, modes, block), F32), ((ITERS, modes), F32)],
        )
    )


def plain_path(
    wide,
    narrow,
    amplitudes,
    integral_slab,
    coupling,
    pair_of_block,
    pair_shift,
    virt_energy,
    core_energy,
    core_index,
    frequency,
    dipole,
):
    virt = virt_energy.shape[0]
    freqs = frequency.shape[0]
    modes = freqs * core_index.shape[0]
    slots = coupling.shape[0]
    block = dipole.shape[1]
    everyone = modes % (wide * narrow) == 0
    group = ("chip", "core", "narrow") if everyone else ("chip", "core")
    members = wide * narrow if everyone else wide
    owned = modes // members

    here = lax.axis_index(("chip", "core", "narrow"))
    mine = lax.axis_index(group)
    picked = jnp.take(dipole, core_index, axis=0)
    picked = lax.all_gather(picked, "narrow", axis=1, tiled=True)
    shift = (frequency[None, :] + jnp.take(core_energy, core_index)[:, None]).reshape(-1)
    offset = jnp.take(pair_shift, lax.dynamic_slice_in_dim(pair_of_block, here * slots, slots))
    rhs = jnp.repeat(picked, freqs, axis=0)
    level = virt_energy[None, :] - shift[:, None]
    mag = level * level + DAMP * DAMP
    response = jnp.concatenate([rhs * level / mag, rhs * DAMP / mag], 0)
    den = shift[None, :, None] - offset[:, None, None] - virt_energy[None, None, :]
    den_mag = den * den + DAMP * DAMP
    own_rhs = lax.dynamic_slice_in_dim(rhs, mine * owned, owned)
    own_level = lax.dynamic_slice_in_dim(level, mine * owned, owned)
    own_mag = own_level * own_level + DAMP * DAMP
    own_re, own_im = own_rhs * own_level / own_mag, own_rhs * DAMP / own_mag
    slab = integral_slab.astype(F32)
    ampl = amplitudes.astype(F32)

    def dot(left, right, dims):
        return lax.dot_general(left, right, dims, precision=HIGHEST, preferred_element_type=F32)

    rms = []
    for sweep in range(ITERS):
        folded = dot(dot(response, slab, LAST), ampl, INNER)
        for slot in range(slots):
            inner = dot(response, coupling[slot], LAST)
            re, im = inner[:modes], inner[modes:]
            quot = jnp.concatenate(
                [
                    (re * den[slot] + im * DAMP) / den_mag[slot],
                    (im * den[slot] - re * DAMP) / den_mag[slot],
                ],
                0,
            )
            folded = folded + dot(quot, coupling[slot], INNER)
        pieces = folded.reshape(2, members, owned, virt).transpose(1, 0, 2, 3)
        total = jnp.sum(lax.all_to_all(pieces, group, 0, 0, tiled=True), 0)
        if not everyone:
            total = lax.psum(total, "narrow")
        res_re = own_rhs - (own_level * own_re + DAMP * own_im + total[0])
        res_im = -(own_level * own_im - DAMP * own_re + total[1])
        squares = jnp.sum(res_re * res_re + res_im * res_im, axis=1)
        rms.append(jnp.sqrt(squares / (2 * virt) + 1e-6))
        own_re = own_re + (res_re * own_level - res_im * DAMP) / own_mag
        own_im = own_im + (res_im * own_level + res_re * DAMP) / own_mag
        own = jnp.stack([own_re, own_im], 0)
        if sweep + 1 < ITERS:
            sent = jnp.broadcast_to(own[None], (members,) + own.shape)
            got = lax.all_to_all(sent, group, 0, 0, tiled=True)
            response = got.transpose(1, 0, 2, 3).reshape(2 * modes, virt)
    if everyone:
        sent = own.reshape(2, owned, narrow, block).transpose(2, 0, 1, 3)
        sent = jnp.broadcast_to(sent[None], (wide,) + sent.shape).reshape(members, 2, owned, block)
    else:
        sent = lax.dynamic_slice_in_dim(own, lax.axis_index("narrow") * block, block, 2)
        sent = jnp.broadcast_to(sent[None], (members,) + sent.shape)
    extra = jnp.broadcast_to(jnp.stack(rms, 0)[None, :, :, None], (members, 2, owned, LANE))
    got = lax.all_to_all(jnp.concatenate([sent, extra], 3), group, 0, 0, tiled=True)
    got = got.transpose(1, 0, 2, 3).reshape(2, modes, block + LANE)
    return got[:, :, :block], got[:, :, block]


def solution(mesh):
    wide, narrow = mesh.shape["wide"], mesh.shape["narrow"]
    chips = wide // 2
    finer = Mesh(mesh.devices.reshape(chips, 2, narrow), ("chip", "core", "narrow"))
    split = ("chip", "core", "narrow")

    def body(*args):
        virt, modes = args[5].shape[0], args[8].shape[0] * args[7].shape[0]
        pieces = (modes // SUB) * (virt // LANE)
        fits = (
            narrow == 2
            and pieces == 2 * chips * narrow
            and modes % (chips * narrow) == 0
            and SUB % (modes // (chips * narrow)) == 0
            and virt % (4 * LANE) == 0
        )
        if fits:
            return fast_path(chips, narrow, *args)
        return plain_path(wide, narrow, *args)

    return jax.shard_map(
        body,
        mesh=finer,
        in_specs=(
            P(split, None),
            P(split, None),
            P(split, None, None),
            P(),
            P(),
            P(),
            P(),
            P(),
            P(),
            P(None, "narrow"),
        ),
        out_specs=(P(None, None, "narrow"), P()),
        check_vma=False,
    )
```

```python
from functools import partial

import jax
import jax.numpy as jnp
from jax import lax
from jax.experimental import pallas as pl
from jax.experimental.pallas import tpu as pltpu
from jax.sharding import Mesh, PartitionSpec as P

ITERS = 2
DAMP = 0.5
HIGHEST = lax.Precision.HIGHEST
F32, BF16 = jnp.float32, jnp.bfloat16
LAST = (((1,), (1,)), ((), ()))
INNER = (((1,), (0,)), ((), ()))
SUB, LANE = 8, 128
VMEM = pl.BlockSpec(memory_space=pltpu.VMEM)
SMEM = pl.BlockSpec(memory_space=pltpu.SMEM)
HBM = pl.BlockSpec(memory_space=pltpu.HBM)
PARTS = 4


def mxu(left, right, dims):
    return lax.dot_general(left, right, dims, preferred_element_type=F32)


def halves(value):
    high = value.astype(BF16)
    return high, (value - high.astype(F32)).astype(BF16)


def stacked(value):
    return jnp.concatenate(halves(value), 0)


def joined(value):
    rows = value.shape[0] // 2
    return value[:rows] + value[rows:]


def call(body, name, operands, in_specs, outs, scratch=(), flops=0, moved=0):
    operands = [
        pltpu.with_memory_space_constraint(x, pltpu.HBM) if spec is HBM else x
        for x, spec in zip(operands, in_specs)
    ]
    return pl.pallas_call(
        body,
        out_shape=[jax.ShapeDtypeStruct(s, d) for s, d in outs],
        in_specs=in_specs,
        out_specs=[VMEM] * len(outs),
        scratch_shapes=scratch,
        name=name,
        compiler_params=pltpu.CompilerParams(vmem_limit_bytes=20 << 20),
        cost_estimate=pl.CostEstimate(flops=flops, bytes_accessed=moved, transcendentals=0),
    )(*operands)


def start_all(pairs, sems):
    copies = [pltpu.make_async_copy(src, dst, sems.at[i]) for i, (src, dst) in enumerate(pairs)]
    for copy in copies:
        copy.start()
    return copies


def pick_body(index_hbm, dipole_hbm, picked, index, dipole, sems):
    copies = start_all([(index_hbm, index), (dipole_hbm, dipole)], sems)
    for copy in copies:
        copy.wait()
    for c in range(index.shape[0]):
        picked[c : c + 1] = dipole[pl.ds(index[c], 1)]


def prepare_body(
    index_hbm,
    energy_hbm,
    frequency_hbm,
    blocks_hbm,
    pair_shift_hbm,
    virt_hbm,
    coupling_hbm,
    slab_hbm,
    level,
    denom,
    high,
    low,
    slab,
    index,
    energy,
    frequency,
    blocks,
    pair_shift,
    virt,
    coupling,
    small_sems,
    coupling_sems,
    slab_sems,
):
    freqs = frequency.shape[0]
    modes, columns = level.shape
    slots = coupling.shape[0]
    small = start_all(
        [
            (index_hbm, index),
            (energy_hbm, energy),
            (frequency_hbm, frequency),
            (blocks_hbm, blocks),
            (pair_shift_hbm, pair_shift),
            (virt_hbm, virt),
        ],
        small_sems,
    )
    step = coupling.shape[1] // PARTS
    parts = [(s, slice(i * step, (i + 1) * step)) for s in range(slots) for i in range(PARTS)]
    coupled = start_all([(coupling_hbm.at[s, r], coupling.at[s, r]) for s, r in parts], coupling_sems)
    step = slab.shape[0] // PARTS
    slabs = start_all(
        [
            (slab_hbm.at[i * step : (i + 1) * step], slab.at[i * step : (i + 1) * step])
            for i in range(PARTS)
        ],
        slab_sems,
    )
    for copy in small:
        copy.wait()
    device = lax.axis_index(("chip", "core", "narrow"))
    rows = lax.broadcasted_iota(jnp.int32, (SUB, LANE), 0)
    tiles = []
    for start in range(0, modes, SUB):
        tile = jnp.zeros((SUB, LANE), F32)
        for k in range(start, start + SUB):
            value = frequency[k % freqs] + energy[index[k // freqs]]
            tile = jnp.where(rows == k - start, value, tile)
        tiles.append(tile)
    shift = jnp.concatenate(tiles, 0)
    for at in range(0, columns, LANE):
        here = jnp.broadcast_to(virt[:, at : at + LANE], (modes, LANE))
        level[:, at : at + LANE] = here - shift
        for s in range(slots):
            offset = pair_shift[blocks[device * slots + s]]
            denom[s, :, at : at + LANE] = (shift - offset) - here
    for (s, r), copy in zip(parts, coupled):
        copy.wait()
        upper, lower = halves(coupling[s, r])
        high[s, r] = upper
        low[s, r] = lower
    for copy in slabs:
        copy.wait()


def fold(response, slab, denom, high, low):
    modes = response.shape[0] // 2
    upper, lower = halves(response)
    both = jnp.concatenate([upper, lower], 0)
    singles = stacked(joined(mxu(both, slab[...], LAST)))
    doubles = []
    for s in range(high.shape[0]):
        inner = joined(mxu(both, high[s], LAST)) + mxu(upper, low[s], LAST)
        re, im = inner[:modes], inner[modes:]
        den = denom[s]
        inverse = 1.0 / (den * den + DAMP * DAMP)
        doubles.append(
            stacked(
                jnp.concatenate(
                    [(re * den + im * DAMP) * inverse, (im * den - re * DAMP) * inverse], 0
                )
            )
        )
    return singles, doubles


def unfold(singles, doubles, amplitudes, high, low, columns):
    total = mxu(singles, amplitudes[:, columns], INNER)
    for s, outgoing in enumerate(doubles):
        total = total + mxu(outgoing, high[s, :, columns], INNER)
    total = joined(total)
    for s, outgoing in enumerate(doubles):
        total = total + mxu(outgoing[: outgoing.shape[0] // 2], low[s, :, columns], INNER)
    return total


def first_body(
    own,
    other,
    level,
    denom,
    high,
    low,
    slab,
    amplitudes_hbm,
    rhs,
    start,
    give,
    keep,
    amplitudes,
    sems,
):
    step = amplitudes.shape[0] // PARTS
    copies = start_all(
        [
            (
                amplitudes_hbm.at[i * step : (i + 1) * step],
                amplitudes.at[i * step : (i + 1) * step],
            )
            for i in range(PARTS)
        ],
        sems,
    )
    modes, virt = level.shape
    cores, block = own.shape
    freqs = modes // cores
    side = lax.axis_index("narrow")
    for part, at in ((own, side), (other, 1 - side)):
        columns = pl.ds(pl.multiple_of(at * block, LANE), block)
        for c in range(cores):
            rhs[c * freqs : (c + 1) * freqs, columns] = jnp.broadcast_to(
                part[c : c + 1], (freqs, block)
            )
    lev = level[...]
    inverse = 1.0 / (lev * lev + DAMP * DAMP)
    start[:modes] = rhs[...] * lev * inverse
    start[modes:] = rhs[...] * DAMP * inverse
    singles, doubles = fold(start[...], slab, denom, high, low)
    for copy in copies:
        copy.wait()
    core = lax.axis_index("core")
    half = virt // 2
    for out, at in ((give, 1 - core), (keep, core)):
        columns = pl.ds(pl.multiple_of(at * half, LANE), half)
        total = unfold(singles, doubles, amplitudes, high, low, columns)
        for group in range(modes // SUB):
            for tile in range(half // LANE):
                piece = group * (half // LANE) + tile
                lanes = slice(tile * LANE, (tile + 1) * LANE)
                out[piece, 0] = total[group * SUB : (group + 1) * SUB, lanes]
                out[piece, 1] = total[modes + group * SUB : modes + (group + 1) * SUB, lanes]


def add_body(left, right, out):
    out[...] = left[...] + right[...]


def first_update_body(got, level, rhs, start, sent):
    members = got.shape[0]
    modes, virt = level.shape
    tiles = virt // 2 // LANE
    mine = lax.axis_index(("chip", "narrow"))
    group, tile = lax.div(mine, tiles), lax.rem(mine, tiles)
    column = lax.axis_index("core") * (virt // 2) + tile * LANE
    columns = pl.ds(pl.multiple_of(column, LANE), LANE)
    rows = pl.ds(pl.multiple_of(group * SUB, SUB), SUB)
    total = got[0]
    for j in range(1, members):
        total = total + got[j]
    lev, right = level[rows, columns], rhs[rows, columns]
    re = start[rows, columns]
    im = start[pl.ds(pl.multiple_of(modes + group * SUB, SUB), SUB), columns]
    inverse = 1.0 / (lev * lev + DAMP * DAMP)
    res_re = right - (lev * re + DAMP * im + total[0])
    res_im = -(lev * im - DAMP * re + total[1])
    re = re + (res_re * lev - res_im * DAMP) * inverse
    im = im + (res_im * lev + res_re * DAMP) * inverse
    for j in range(members):
        sent[j, 0] = re
        sent[j, 1] = im


def second_body(
    own, other, level, denom, high, low, slab, amplitudes, response, give, keep
):
    modes, virt = level.shape
    members = own.shape[0]
    half, quarter = virt // 2, virt // 4
    core = lax.axis_index("core")
    for part, at in ((own, core), (other, 1 - core)):
        for group in range(modes // SUB):
            for tile in range(half // LANE):
                piece = group * (half // LANE) + tile
                columns = pl.ds(pl.multiple_of(at * half + tile * LANE, LANE), LANE)
                response[group * SUB : (group + 1) * SUB, columns] = part[piece, 0]
                response[modes + group * SUB : modes + (group + 1) * SUB, columns] = part[piece, 1]
    singles, doubles = fold(response[...], slab, denom, high, low)
    owned = modes // members
    for out, at in ((give, 1 - core), (keep, core)):
        for side in range(2):
            columns = pl.ds(pl.multiple_of(side * half + at * quarter, LANE), quarter)
            total = unfold(singles, doubles, amplitudes, high, low, columns)
            lanes = slice(side * quarter, (side + 1) * quarter)
            for j in range(members):
                out[j, :owned, lanes] = total[j * owned : (j + 1) * owned]
                out[j, owned:, lanes] = total[modes + j * owned : modes + (j + 1) * owned]


def second_update_body(got, level, rhs, start, response, sent):
    members, double, width = got.shape
    owned = double // 2
    modes, virt = level.shape
    half, quarter = virt // 2, virt // 4
    mine = lax.axis_index(("chip", "narrow"))
    core = lax.axis_index("core")
    total = got[0]
    for j in range(1, members):
        total = total + got[j]
    per_tile = SUB // owned
    within = lax.rem(mine, per_tile)

    def own_rows(ref, first, columns):
        at = first + lax.div(mine, per_tile) * SUB
        tile = ref[pl.ds(pl.multiple_of(at, SUB), SUB), columns]
        rows = tile[:owned]
        for q in range(1, per_tile):
            rows = jnp.where(within == q, tile[q * owned : (q + 1) * owned], rows)
        return rows

    old_squares = jnp.zeros((owned, 1), F32)
    new_squares = jnp.zeros((owned, 1), F32)
    fresh = []
    for side in range(2):
        columns = pl.ds(pl.multiple_of(side * half + core * quarter, LANE), quarter)
        lanes = slice(side * quarter, (side + 1) * quarter)
        lev, right = own_rows(level, 0, columns), own_rows(rhs, 0, columns)
        re, im = own_rows(response, 0, columns), own_rows(response, modes, columns)
        step_re = re - own_rows(start, 0, columns)
        step_im = im - own_rows(start, modes, columns)
        old_re = lev * step_re + DAMP * step_im
        old_im = lev * step_im - DAMP * step_re
        old_squares += jnp.sum(old_re * old_re + old_im * old_im, axis=1, keepdims=True)
        inverse = 1.0 / (lev * lev + DAMP * DAMP)
        res_re = right - (lev * re + DAMP * im + total[:owned, lanes])
        res_im = -(lev * im - DAMP * re + total[owned:, lanes])
        new_squares += jnp.sum(res_re * res_re + res_im * res_im, axis=1, keepdims=True)
        re = re + (res_re * lev - res_im * DAMP) * inverse
        im = im + (res_im * lev + res_re * DAMP) * inverse
        fresh.append((re, im))
    squares = jnp.concatenate([old_squares, new_squares], 0)
    for j in range(members):
        re, im = fresh[j % 2]
        sent[j, :owned, :quarter] = re
        sent[j, owned:, :quarter] = im
        sent[j, :, quarter:] = jnp.broadcast_to(squares, (double, LANE))


def finish_body(own, other, response, rms):
    members, double, _ = own.shape
    owned = double // 2
    quarter = response.shape[2] // 2
    sweeps, modes = rms.shape
    core = lax.axis_index("core")
    for part, at in ((own, core), (other, 1 - core)):
        columns = pl.ds(pl.multiple_of(at * quarter, LANE), quarter)
        for j in range(members):
            for q in range(2):
                response[q, j * owned : (j + 1) * owned, columns] = part[
                    j, q * owned : (q + 1) * owned, :quarter
                ]
    row = lax.broadcasted_iota(jnp.int32, (sweeps, LANE), 0)
    lane = lax.broadcasted_iota(jnp.int32, (sweeps, LANE), 1)
    squares = jnp.zeros((sweeps, LANE), F32)
    for j in range(members):
        both = own[j, :, quarter:] + other[j, :, quarter:]
        for s in range(sweeps):
            for i in range(owned):
                at = s * owned + i
                value = jnp.broadcast_to(both[at : at + 1], (sweeps, LANE))
                squares = jnp.where((row == s) & (lane == j * owned + i), value, squares)
    virt = 4 * quarter
    rms[...] = jnp.sqrt(squares / (2 * virt) + 1e-6)[:, :modes]


def fast_path(
    chips,
    narrow,
    amplitudes,
    integral_slab,
    coupling,
    pair_of_block,
    pair_shift,
    virt_energy,
    core_energy,
    core_index,
    frequency,
    dipole,
):
    virt = virt_energy.shape[0]
    cores = core_index.shape[0]
    modes = frequency.shape[0] * cores
    slots = coupling.shape[0]
    block = dipole.shape[1]
    rows = amplitudes.shape[0]
    members = chips * narrow
    half = virt // 2
    flip_core = [(0, 1), (1, 0)]
    group = ("chip", "narrow")
    cost = dict(flops=8 * modes * virt * (virt * slots + rows), moved=4 * virt * (virt * slots + rows))

    (picked,) = call(
        pick_body,
        "pick",
        (core_index, dipole),
        [HBM, HBM],
        [((cores, block), F32)],
        scratch=[
            pltpu.SMEM(core_index.shape, jnp.int32),
            pltpu.VMEM(dipole.shape, F32),
            pltpu.SemaphoreType.DMA((2,)),
        ],
        moved=cores * block * 4,
    )
    across = lax.ppermute(picked, "narrow", flip_core)
    scalars = (core_index, core_energy, frequency, pair_of_block, pair_shift)
    level, denom, high, low, slab = call(
        prepare_body,
        "prepare",
        scalars + (virt_energy[None], coupling, integral_slab),
        [HBM] * 8,
        [
            ((modes, virt), F32),
            ((slots, modes, virt), F32),
            ((slots, virt, virt), BF16),
            ((slots, virt, virt), BF16),
            (integral_slab.shape, BF16),
        ],
        scratch=[pltpu.SMEM(a.shape, a.dtype) for a in scalars]
        + [
            pltpu.VMEM((1, virt), F32),
            pltpu.VMEM(coupling.shape, F32),
            pltpu.SemaphoreType.DMA((6,)),
            pltpu.SemaphoreType.DMA((PARTS * slots,)),
            pltpu.SemaphoreType.DMA((PARTS,)),
        ],
        flops=4 * slots * virt * virt,
        moved=8 * slots * virt * virt,
    )
    piece = (members, 2, SUB, LANE)
    rhs, start, give, keep, held = call(
        first_body,
        "first",
        (picked, across, level, denom, high, low, slab, amplitudes),
        [VMEM] * 7 + [HBM],
        [
            ((modes, virt), F32),
            ((2 * modes, virt), F32),
            (piece, F32),
            (piece, F32),
            (amplitudes.shape, BF16),
        ],
        scratch=[pltpu.SemaphoreType.DMA((PARTS,))],
        **cost,
    )
    got = lax.ppermute(give, "core", flip_core)
    (total,) = call(add_body, "add_first", (keep, got), [VMEM] * 2, [(piece, F32)])
    got = lax.all_to_all(total, group, 0, 0, tiled=True)
    (sent,) = call(
        first_update_body, "first_update", (got, level, rhs, start), [VMEM] * 4, [(piece, F32)]
    )
    got = lax.all_to_all(sent, group, 0, 0, tiled=True)
    other = lax.ppermute(got, "core", flip_core)
    owned = modes // members
    piece = (members, 2 * owned, half)
    response, give, keep = call(
        second_body,
        "second",
        (got, other, level, denom, high, low, slab, held),
        [VMEM] * 8,
        [((2 * modes, virt), F32), (piece, F32), (piece, F32)],
        **cost,
    )
    got = lax.ppermute(give, "core", flip_core)
    (total,) = call(add_body, "add_second", (keep, got), [VMEM] * 2, [(piece, F32)])
    got = lax.all_to_all(total, group, 0, 0, tiled=True)
    piece = (members, 2 * owned, half // 2 + LANE)
    (sent,) = call(
        second_update_body,
        "second_update",
        (got, level, rhs, start, response),
        [VMEM] * 5,
        [(piece, F32)],
    )
    got = lax.all_to_all(sent, group, 0, 0, tiled=True)
    other = lax.ppermute(got, "core", flip_core)
    return tuple(
        call(
            finish_body,
            "finish",
            (got, other),
            [VMEM] * 2,
            [((2, modes, block), F32), ((ITERS, modes), F32)],
        )
    )


def plain_path(
    wide,
    narrow,
    amplitudes,
    integral_slab,
    coupling,
    pair_of_block,
    pair_shift,
    virt_energy,
    core_energy,
    core_index,
    frequency,
    dipole,
):
    virt = virt_energy.shape[0]
    freqs = frequency.shape[0]
    modes = freqs * core_index.shape[0]
    slots = coupling.shape[0]
    block = dipole.shape[1]
    everyone = modes % (wide * narrow) == 0
    group = ("chip", "core", "narrow") if everyone else ("chip", "core")
    members = wide * narrow if everyone else wide
    owned = modes // members

    here = lax.axis_index(("chip", "core", "narrow"))
    mine = lax.axis_index(group)
    picked = jnp.take(dipole, core_index, axis=0)
    picked = lax.all_gather(picked, "narrow", axis=1, tiled=True)
    shift = (frequency[None, :] + jnp.take(core_energy, core_index)[:, None]).reshape(-1)
    offset = jnp.take(pair_shift, lax.dynamic_slice_in_dim(pair_of_block, here * slots, slots))
    rhs = jnp.repeat(picked, freqs, axis=0)
    level = virt_energy[None, :] - shift[:, None]
    mag = level * level + DAMP * DAMP
    response = jnp.concatenate([rhs * level / mag, rhs * DAMP / mag], 0)
    den = shift[None, :, None] - offset[:, None, None] - virt_energy[None, None, :]
    den_mag = den * den + DAMP * DAMP
    own_rhs = lax.dynamic_slice_in_dim(rhs, mine * owned, owned)
    own_level = lax.dynamic_slice_in_dim(level, mine * owned, owned)
    own_mag = own_level * own_level + DAMP * DAMP
    own_re, own_im = own_rhs * own_level / own_mag, own_rhs * DAMP / own_mag
    slab = integral_slab.astype(F32)
    ampl = amplitudes.astype(F32)

    def dot(left, right, dims):
        return lax.dot_general(left, right, dims, precision=HIGHEST, preferred_element_type=F32)

    rms = []
    for sweep in range(ITERS):
        folded = dot(dot(response, slab, LAST), ampl, INNER)
        for slot in range(slots):
            inner = dot(response, coupling[slot], LAST)
            re, im = inner[:modes], inner[modes:]
            quot = jnp.concatenate(
                [
                    (re * den[slot] + im * DAMP) / den_mag[slot],
                    (im * den[slot] - re * DAMP) / den_mag[slot],
                ],
                0,
            )
            folded = folded + dot(quot, coupling[slot], INNER)
        pieces = folded.reshape(2, members, owned, virt).transpose(1, 0, 2, 3)
        total = jnp.sum(lax.all_to_all(pieces, group, 0, 0, tiled=True), 0)
        if not everyone:
            total = lax.psum(total, "narrow")
        res_re = own_rhs - (own_level * own_re + DAMP * own_im + total[0])
        res_im = -(own_level * own_im - DAMP * own_re + total[1])
        squares = jnp.sum(res_re * res_re + res_im * res_im, axis=1)
        rms.append(jnp.sqrt(squares / (2 * virt) + 1e-6))
        own_re = own_re + (res_re * own_level - res_im * DAMP) / own_mag
        own_im = own_im + (res_im * own_level + res_re * DAMP) / own_mag
        own = jnp.stack([own_re, own_im], 0)
        if sweep + 1 < ITERS:
            sent = jnp.broadcast_to(own[None], (members,) + own.shape)
            got = lax.all_to_all(sent, group, 0, 0, tiled=True)
            response = got.transpose(1, 0, 2, 3).reshape(2 * modes, virt)
    if everyone:
        sent = own.reshape(2, owned, narrow, block).transpose(2, 0, 1, 3)
        sent = jnp.broadcast_to(sent[None], (wide,) + sent.shape).reshape(members, 2, owned, block)
    else:
        sent = lax.dynamic_slice_in_dim(own, lax.axis_index("narrow") * block, block, 2)
        sent = jnp.broadcast_to(sent[None], (members,) + sent.shape)
    extra = jnp.broadcast_to(jnp.stack(rms, 0)[None, :, :, None], (members, 2, owned, LANE))
    got = lax.all_to_all(jnp.concatenate([sent, extra], 3), group, 0, 0, tiled=True)
    got = got.transpose(1, 0, 2, 3).reshape(2, modes, block + LANE)
    return got[:, :, :block], got[:, :, block]


def solution(mesh):
    wide, narrow = mesh.shape["wide"], mesh.shape["narrow"]
    chips = wide // 2
    finer = Mesh(mesh.devices.reshape(chips, 2, narrow), ("chip", "core", "narrow"))
    split = ("chip", "core", "narrow")

    def body(*args):
        virt, modes = args[5].shape[0], args[8].shape[0] * args[7].shape[0]
        pieces = (modes // SUB) * (virt // LANE)
        fits = (
            narrow == 2
            and pieces == 2 * chips * narrow
            and modes % (chips * narrow) == 0
            and SUB % (modes // (chips * narrow)) == 0
            and virt % (4 * LANE) == 0
        )
        if fits:
            return fast_path(chips, narrow, *args)
        return plain_path(wide, narrow, *args)

    return jax.shard_map(
        body,
        mesh=finer,
        in_specs=(
            P(split, None),
            P(split, None),
            P(split, None, None),
            P(),
            P(),
            P(),
            P(),
            P(),
            P(),
            P(None, "narrow"),
        ),
        out_specs=(P(None, None, "narrow"), P()),
        check_vma=False,
    )
```

```python
from functools import partial

import jax
import jax.numpy as jnp
from jax import lax
from jax.experimental import pallas as pl
from jax.experimental.pallas import tpu as pltpu
from jax.sharding import Mesh, PartitionSpec as P

ITERS = 2
DAMP = 0.5
HIGHEST = lax.Precision.HIGHEST
F32, BF16 = jnp.float32, jnp.bfloat16
LAST = (((1,), (1,)), ((), ()))
INNER = (((1,), (0,)), ((), ()))
SUB, LANE = 8, 128
VMEM = pl.BlockSpec(memory_space=pltpu.VMEM)
SMEM = pl.BlockSpec(memory_space=pltpu.SMEM)
HBM = pl.BlockSpec(memory_space=pltpu.HBM)
PARTS = 8
WINDOW = 11


def mxu(left, right, dims):
    return lax.dot_general(left, right, dims, preferred_element_type=F32)


def halves(value):
    high = value.astype(BF16)
    return high, (value - high.astype(F32)).astype(BF16)


def stacked(value):
    return jnp.concatenate(halves(value), 0)


def joined(value):
    rows = value.shape[0] // 2
    return value[:rows] + value[rows:]


def call(body, name, operands, in_specs, outs, scratch=(), flops=0, moved=0):
    operands = [
        pltpu.with_memory_space_constraint(x, pltpu.HBM) if spec is HBM else x
        for x, spec in zip(operands, in_specs)
    ]
    return pl.pallas_call(
        body,
        out_shape=[jax.ShapeDtypeStruct(s, d) for s, d in outs],
        in_specs=in_specs,
        out_specs=[VMEM] * len(outs),
        scratch_shapes=scratch,
        name=name,
        compiler_params=pltpu.CompilerParams(vmem_limit_bytes=20 << 20),
        cost_estimate=pl.CostEstimate(flops=flops, bytes_accessed=moved, transcendentals=0),
    )(*operands)


def start_all(pairs, sems):
    copies = [pltpu.make_async_copy(src, dst, sems.at[i]) for i, (src, dst) in enumerate(pairs)]
    for copy in copies:
        copy.start()
    return copies


def prepare_body(
    index_hbm,
    energy_hbm,
    frequency_hbm,
    blocks_hbm,
    pair_shift_hbm,
    virt_hbm,
    dipole_hbm,
    coupling_hbm,
    slab_hbm,
    picked,
    chosen,
    level,
    denom,
    high,
    low,
    slab_t,
    index,
    energy,
    frequency,
    blocks,
    pair_shift,
    virt,
    dipole,
    coupling,
    slab,
    small_sems,
    coupling_sems,
    slab_sems,
):
    freqs = frequency.shape[0]
    modes, columns = level.shape
    slots = coupling.shape[0]
    small = start_all(
        [
            (index_hbm, index),
            (energy_hbm, energy),
            (frequency_hbm, frequency),
            (blocks_hbm, blocks),
            (pair_shift_hbm, pair_shift),
            (virt_hbm, virt),
            (dipole_hbm, dipole),
        ],
        small_sems,
    )
    step = coupling.shape[1] // PARTS
    parts = [(s, slice(i * step, (i + 1) * step)) for s in range(slots) for i in range(PARTS)]
    coupled = [
        pltpu.make_async_copy(coupling_hbm.at[s, r], coupling.at[s, r], coupling_sems.at[i])
        for i, (s, r) in enumerate(parts)
    ]
    step = slab.shape[0] // PARTS
    pieces = [slice(i * step, (i + 1) * step) for i in range(PARTS)]
    slabs = [
        pltpu.make_async_copy(slab_hbm.at[r], slab.at[r], slab_sems.at[i])
        for i, r in enumerate(pieces)
    ]
    waiting = coupled + slabs

    def advance(count):
        for copy in waiting[:count]:
            copy.start()
        del waiting[:count]

    advance(WINDOW)
    for copy in small:
        copy.wait()
    orbital = lax.broadcasted_iota(jnp.int32, chosen.shape[1:], 0)
    for c in range(index.shape[0]):
        picked[c : c + 1] = dipole[pl.ds(index[c], 1)]
        chosen[c] = jnp.where(orbital == index[c], 1.0, 0.0)
    device = lax.axis_index(("chip", "core", "narrow"))
    rows = lax.broadcasted_iota(jnp.int32, (SUB, LANE), 0)
    tiles = []
    for start in range(0, modes, SUB):
        tile = jnp.zeros((SUB, LANE), F32)
        for k in range(start, start + SUB):
            value = frequency[k % freqs] + energy[index[k // freqs]]
            tile = jnp.where(rows == k - start, value, tile)
        tiles.append(tile)
    shift = jnp.concatenate(tiles, 0)
    for at in range(0, columns, LANE):
        here = jnp.broadcast_to(virt[:, at : at + LANE], (modes, LANE))
        level[:, at : at + LANE] = here - shift
        for s in range(slots):
            offset = pair_shift[blocks[device * slots + s]]
            denom[s, :, at : at + LANE] = (shift - offset) - here
    for (s, r), copy in zip(parts, coupled):
        copy.wait()
        advance(1)
        upper, lower = halves(coupling[s, r])
        high[s, r] = upper
        low[s, r] = lower
    for r, copy in zip(pieces, slabs):
        copy.wait()
        advance(1)
        slab_t[:, r] = slab[r].T


def fold(response, slab_t, high, low, dims):
    upper, lower = halves(response)
    both = jnp.concatenate([upper, lower], 0)
    singles = joined(mxu(both, slab_t, INNER))
    doubles = [joined(mxu(both, h, dims)) + mxu(upper, l, dims) for h, l in zip(high, low)]
    return singles, doubles


def quotient(inner, den):
    modes = den.shape[0]
    re, im = inner[:modes], inner[modes:]
    inverse = 1.0 / (den * den + DAMP * DAMP)
    return jnp.concatenate(
        [(re * den + im * DAMP) * inverse, (im * den - re * DAMP) * inverse], 0
    )


def unfold(singles, doubles, amplitudes, high, low, columns):
    total = mxu(singles[...], amplitudes[:, columns], INNER)
    slots, double = doubles.shape[:2]
    for s in range(slots):
        total = total + mxu(doubles[s], high[s, :, columns], INNER)
    total = joined(total)
    for s in range(slots):
        total = total + mxu(doubles[s, : double // 2], low[s, :, columns], INNER)
    return total


def write_tiles(out, total, modes):
    tiles = total.shape[1] // LANE
    for group in range(modes // SUB):
        for tile in range(tiles):
            piece, lanes = group * tiles + tile, slice(tile * LANE, (tile + 1) * LANE)
            out[piece, 0] = total[group * SUB : (group + 1) * SUB, lanes]
            out[piece, 1] = total[modes + group * SUB : modes + (group + 1) * SUB, lanes]


def first_body(
    own,
    other,
    chosen,
    level,
    denom,
    high,
    low,
    slab_t,
    amplitudes_hbm,
    rhs,
    start,
    singles,
    doubles,
    give,
    amplitudes,
    sems,
):
    step = amplitudes.shape[0] // PARTS
    copies = start_all(
        [
            (
                amplitudes_hbm.at[i * step : (i + 1) * step],
                amplitudes.at[i * step : (i + 1) * step],
            )
            for i in range(PARTS)
        ],
        sems,
    )
    modes, virt = level.shape
    cores, block = own.shape
    freqs = modes // cores
    side = lax.axis_index("narrow")
    here = pl.ds(pl.multiple_of(side * block, LANE), block)
    there = pl.ds(pl.multiple_of((1 - side) * block, LANE), block)
    for c in range(cores):
        span = slice(c * freqs, (c + 1) * freqs)
        mask = jnp.concatenate([chosen[c]] * (block // LANE), 1)
        theirs = jnp.sum(jnp.where(mask > 0.5, other[...], 0.0), axis=0, keepdims=True)
        rhs[span, here] = jnp.broadcast_to(own[c : c + 1], (freqs, block))
        rhs[span, there] = jnp.broadcast_to(theirs, (freqs, block))
    lev = level[...]
    inverse = 1.0 / (lev * lev + DAMP * DAMP)
    start[:modes] = rhs[...] * lev * inverse
    start[modes:] = rhs[...] * DAMP * inverse
    slots = range(high.shape[0])
    single, inner = fold(
        start[...], slab_t[...], [high[s] for s in slots], [low[s] for s in slots], LAST
    )
    singles[...] = stacked(single)
    for s, value in enumerate(inner):
        doubles[s] = stacked(quotient(value, denom[s]))
    for copy in copies:
        copy.wait()
    columns = pl.ds(pl.multiple_of((1 - lax.axis_index("core")) * (virt // 2), LANE), virt // 2)
    write_tiles(give, unfold(singles, doubles, amplitudes, high, low, columns), modes)


def first_rest_body(singles, doubles, amplitudes, high, low, keep, high_t, low_t):
    modes, half = singles.shape[0] // 4, high.shape[2] // 2
    core = lax.axis_index("core")
    columns = pl.ds(pl.multiple_of(core * half, LANE), half)
    rest = pl.ds(pl.multiple_of((1 - core) * half, LANE), half)
    write_tiles(keep, unfold(singles, doubles, amplitudes, high, low, columns), modes)
    for s in range(high.shape[0]):
        high_t[s] = high[s, :, rest].T
        low_t[s] = low[s, :, rest].T


def add_body(left, right, out):
    out[...] = left[...] + right[...]


def first_update_body(got, level, rhs, start, sent):
    members = got.shape[0]
    modes, virt = level.shape
    tiles = virt // 2 // LANE
    mine = lax.axis_index(("chip", "narrow"))
    group, tile = lax.div(mine, tiles), lax.rem(mine, tiles)
    column = lax.axis_index("core") * (virt // 2) + tile * LANE
    columns = pl.ds(pl.multiple_of(column, LANE), LANE)
    rows = pl.ds(pl.multiple_of(group * SUB, SUB), SUB)
    total = got[0]
    for j in range(1, members):
        total = total + got[j]
    lev, right = level[rows, columns], rhs[rows, columns]
    re = start[rows, columns]
    im = start[pl.ds(pl.multiple_of(modes + group * SUB, SUB), SUB), columns]
    inverse = 1.0 / (lev * lev + DAMP * DAMP)
    res_re = right - (lev * re + DAMP * im + total[0])
    res_im = -(lev * im - DAMP * re + total[1])
    re = re + (res_re * lev - res_im * DAMP) * inverse
    im = im + (res_im * lev + res_re * DAMP) * inverse
    for j in range(members):
        sent[j, 0] = re
        sent[j, 1] = im


def read_tiles(part, modes):
    tiles = part.shape[0] // (modes // SUB)
    rows = [
        jnp.concatenate([part[group * tiles + tile, q] for tile in range(tiles)], 1)
        for q in range(2)
        for group in range(modes // SUB)
    ]
    return jnp.concatenate(rows, 0)


def second_own_body(own, slab_t, high, low, response, singles, doubles):
    modes, half = response.shape[0] // 2, response.shape[1]
    mine = pl.ds(pl.multiple_of(lax.axis_index("core") * half, LANE), half)
    slots = range(high.shape[0])
    response[...] = read_tiles(own, modes)
    single, inner = fold(
        response[...],
        slab_t[mine],
        [high[s, :, mine] for s in slots],
        [low[s, :, mine] for s in slots],
        LAST,
    )
    singles[...] = single
    for s, value in enumerate(inner):
        doubles[s] = value


def write_owned(out, singles, doubles, amplitudes, high, low, at):
    members, double, half = out.shape
    owned, quarter = double // 2, half // 2
    modes = members * owned
    for side in range(2):
        columns = pl.ds(pl.multiple_of(side * half + at * quarter, LANE), quarter)
        total = unfold(singles, doubles, amplitudes, high, low, columns)
        lanes = slice(side * quarter, (side + 1) * quarter)
        for j in range(members):
            out[j, :owned, lanes] = total[j * owned : (j + 1) * owned]
            out[j, owned:, lanes] = total[modes + j * owned : modes + (j + 1) * owned]


def second_body(
    mine,
    other,
    single_part,
    double_part,
    denom,
    high,
    low,
    high_t,
    low_t,
    slab_t,
    amplitudes,
    response,
    singles,
    doubles,
    give,
):
    half = mine.shape[1]
    modes = mine.shape[0] // 2
    core = lax.axis_index("core")
    columns = pl.ds(pl.multiple_of(core * half, LANE), half)
    rest = pl.ds(pl.multiple_of((1 - core) * half, LANE), half)
    theirs = read_tiles(other, modes)
    response[:, columns] = mine[...]
    response[:, rest] = theirs
    slots = range(high_t.shape[0])
    single, inner = fold(
        theirs, slab_t[rest], [high_t[s] for s in slots], [low_t[s] for s in slots], INNER
    )
    singles[...] = stacked(single_part[...] + single)
    for s, value in enumerate(inner):
        doubles[s] = stacked(quotient(double_part[s] + value, denom[s]))
    write_owned(give, singles, doubles, amplitudes, high, low, 1 - core)


def second_rest_body(singles, doubles, amplitudes, high, low, keep):
    write_owned(keep, singles, doubles, amplitudes, high, low, lax.axis_index("core"))


def second_update_body(got, level, rhs, response, sent):
    members, double, width = got.shape
    owned = double // 2
    modes, virt = level.shape
    half, quarter = virt // 2, virt // 4
    mine = lax.axis_index(("chip", "narrow"))
    core = lax.axis_index("core")
    total = got[0]
    for j in range(1, members):
        total = total + got[j]
    per_tile = SUB // owned
    within = lax.rem(mine, per_tile)

    def own_rows(ref, first, columns):
        at = first + lax.div(mine, per_tile) * SUB
        tile = ref[pl.ds(pl.multiple_of(at, SUB), SUB), columns]
        rows = tile[:owned]
        for q in range(1, per_tile):
            rows = jnp.where(within == q, tile[q * owned : (q + 1) * owned], rows)
        return rows

    squares = jnp.zeros((owned, 1), F32)
    fresh = []
    for side in range(2):
        columns = pl.ds(pl.multiple_of(side * half + core * quarter, LANE), quarter)
        lanes = slice(side * quarter, (side + 1) * quarter)
        lev, right = own_rows(level, 0, columns), own_rows(rhs, 0, columns)
        re, im = own_rows(response, 0, columns), own_rows(response, modes, columns)
        inverse = 1.0 / (lev * lev + DAMP * DAMP)
        res_re = right - (lev * re + DAMP * im + total[:owned, lanes])
        res_im = -(lev * im - DAMP * re + total[owned:, lanes])
        squares += jnp.sum(res_re * res_re + res_im * res_im, axis=1, keepdims=True)
        re = re + (res_re * lev - res_im * DAMP) * inverse
        im = im + (res_im * lev + res_re * DAMP) * inverse
        fresh.append(jnp.concatenate([re, im], 0))
    lane = lax.broadcasted_iota(jnp.int32, (1, LANE), 1)
    tail = jnp.zeros((1, LANE), F32)
    for i in range(owned):
        tail = jnp.where(lane == i, jnp.broadcast_to(squares[i : i + 1], (1, LANE)), tail)
    for j in range(members):
        for i in range(double):
            sent[j, :, i * quarter : (i + 1) * quarter] = fresh[j % 2][i : i + 1]
        sent[j, :, double * quarter :] = tail


def old_squares_body(level, start, response, out):
    modes = level.shape[0]
    lev = level[...]
    re = response[:modes] - start[:modes]
    im = response[modes:] - start[modes:]
    res_re = lev * re + DAMP * im
    res_im = lev * im - DAMP * re
    out[...] = jnp.sum(res_re * res_re + res_im * res_im, axis=1, keepdims=True)


def finish_body(own, other, old, response, rms):
    members = own.shape[0]
    quarter = response.shape[2] // 2
    sweeps, modes = rms.shape
    owned = modes // members
    double = 2 * owned
    core = lax.axis_index("core")
    for part, at in ((own, core), (other, 1 - core)):
        columns = pl.ds(pl.multiple_of(at * quarter, LANE), quarter)
        for j in range(members):
            for i in range(double):
                k = j * owned + i % owned
                response[i // owned, k : k + 1, columns] = part[
                    j, :, i * quarter : (i + 1) * quarter
                ]
    row = lax.broadcasted_iota(jnp.int32, (sweeps, LANE), 0)
    lane = lax.broadcasted_iota(jnp.int32, (sweeps, LANE), 1)
    squares = jnp.zeros((sweeps, LANE), F32)
    for j in range(members):
        both = own[j, :, double * quarter :] + other[j, :, double * quarter :]
        for i in range(owned):
            k = j * owned + i
            value = jnp.broadcast_to(both[:, i : i + 1], (sweeps, LANE))
            squares = jnp.where((row == 1) & (lane == k), value, squares)
            value = jnp.broadcast_to(old[k : k + 1], (sweeps, LANE))
            squares = jnp.where((row == 0) & (lane == k), value, squares)
    virt = 4 * quarter
    rms[...] = jnp.sqrt(squares / (2 * virt) + 1e-6)[:, :modes]


def fast_path(
    chips,
    narrow,
    amplitudes,
    integral_slab,
    coupling,
    pair_of_block,
    pair_shift,
    virt_energy,
    core_energy,
    core_index,
    frequency,
    dipole,
):
    virt = virt_energy.shape[0]
    cores = core_index.shape[0]
    modes = frequency.shape[0] * cores
    slots = coupling.shape[0]
    block = dipole.shape[1]
    rows = amplitudes.shape[0]
    members = chips * narrow
    half = virt // 2
    flip_core = [(0, 1), (1, 0)]
    group = ("chip", "narrow")
    work = 8 * modes * virt * (virt * slots + rows)
    size = 2 * virt * (2 * virt * slots + rows)

    across = lax.ppermute(dipole, "narrow", flip_core)
    scalars = (core_index, core_energy, frequency, pair_of_block, pair_shift)
    picked, chosen, level, denom, high, low, slab_t = call(
        prepare_body,
        "prepare",
        scalars + (virt_energy[None], dipole, coupling, integral_slab),
        [HBM] * 9,
        [((cores, block), F32), ((cores, dipole.shape[0], LANE), F32)]
        + [((modes, virt), F32), ((slots, modes, virt), F32)]
        + [((slots, virt, virt), BF16)] * 2
        + [((virt, rows), BF16)],
        scratch=[pltpu.SMEM(a.shape, a.dtype) for a in scalars]
        + [
            pltpu.VMEM((1, virt), F32),
            pltpu.VMEM(dipole.shape, F32),
            pltpu.VMEM(coupling.shape, F32),
            pltpu.VMEM(integral_slab.shape, BF16),
            pltpu.SemaphoreType.DMA((7,)),
            pltpu.SemaphoreType.DMA((PARTS * slots,)),
            pltpu.SemaphoreType.DMA((PARTS,)),
        ],
        flops=4 * slots * virt * virt,
        moved=2 * size,
    )
    piece = (members, 2, SUB, LANE)
    between = [((4 * modes, rows), BF16), ((slots, 4 * modes, virt), BF16)]
    rhs, start, singles, doubles, give, held = call(
        first_body,
        "first",
        (picked, across, chosen, level, denom, high, low, slab_t, amplitudes),
        [VMEM] * 8 + [HBM],
        [((modes, virt), F32), ((2 * modes, virt), F32)]
        + between
        + [(piece, F32), (amplitudes.shape, BF16)],
        scratch=[pltpu.SemaphoreType.DMA((PARTS,))],
        flops=work * 3 // 4,
        moved=2 * size,
    )
    got = lax.ppermute(give, "core", flip_core)
    keep, high_t, low_t = call(
        first_rest_body,
        "first_rest",
        (singles, doubles, held, high, low),
        [VMEM] * 5,
        [(piece, F32)] + [((slots, half, virt), BF16)] * 2,
        flops=work // 4,
        moved=size // 2,
    )
    (total,) = call(add_body, "add_first", (keep, got), [VMEM] * 2, [(piece, F32)])
    got = lax.all_to_all(total, group, 0, 0, tiled=True)
    (sent,) = call(
        first_update_body, "first_update", (got, level, rhs, start), [VMEM] * 4, [(piece, F32)]
    )
    got = lax.all_to_all(sent, group, 0, 0, tiled=True)
    other = lax.ppermute(got, "core", flip_core)
    owned = modes // members
    piece = (members, 2 * owned, half)
    mine, single_part, double_part = call(
        second_own_body,
        "second_own",
        (got, slab_t, high, low),
        [VMEM] * 4,
        [
            ((2 * modes, half), F32),
            ((2 * modes, rows), F32),
            ((slots, 2 * modes, virt), F32),
        ],
        flops=work // 4,
        moved=size // 2,
    )
    response, singles, doubles, give = call(
        second_body,
        "second",
        (mine, other, single_part, double_part, denom, high, low, high_t, low_t, slab_t, held),
        [VMEM] * 11,
        [((2 * modes, virt), F32)] + between + [(piece, F32)],
        flops=work // 2,
        moved=size,
    )
    got = lax.ppermute(give, "core", flip_core)
    (keep,) = call(
        second_rest_body,
        "second_rest",
        (singles, doubles, held, high, low),
        [VMEM] * 5,
        [(piece, F32)],
        flops=work // 4,
        moved=size // 2,
    )
    (total,) = call(add_body, "add_second", (keep, got), [VMEM] * 2, [(piece, F32)])
    got = lax.all_to_all(total, group, 0, 0, tiled=True)
    piece = (members, 1, owned * virt // 2 + LANE)
    (sent,) = call(
        second_update_body,
        "second_update",
        (got, level, rhs, response),
        [VMEM] * 4,
        [(piece, F32)],
    )
    got = lax.all_to_all(sent, group, 0, 0, tiled=True)
    other = lax.ppermute(got, "core", flip_core)
    (old,) = call(
        old_squares_body, "old_squares", (level, start, response), [VMEM] * 3, [((modes, 1), F32)]
    )
    return tuple(
        call(
            finish_body,
            "finish",
            (got, other, old),
            [VMEM] * 3,
            [((2, modes, block), F32), ((ITERS, modes), F32)],
        )
    )


def plain_path(
    wide,
    narrow,
    amplitudes,
    integral_slab,
    coupling,
    pair_of_block,
    pair_shift,
    virt_energy,
    core_energy,
    core_index,
    frequency,
    dipole,
):
    virt = virt_energy.shape[0]
    freqs = frequency.shape[0]
    modes = freqs * core_index.shape[0]
    slots = coupling.shape[0]
    block = dipole.shape[1]
    everyone = modes % (wide * narrow) == 0
    group = ("chip", "core", "narrow") if everyone else ("chip", "core")
    members = wide * narrow if everyone else wide
    owned = modes // members

    here = lax.axis_index(("chip", "core", "narrow"))
    mine = lax.axis_index(group)
    picked = jnp.take(dipole, core_index, axis=0)
    picked = lax.all_gather(picked, "narrow", axis=1, tiled=True)
    shift = (frequency[None, :] + jnp.take(core_energy, core_index)[:, None]).reshape(-1)
    offset = jnp.take(pair_shift, lax.dynamic_slice_in_dim(pair_of_block, here * slots, slots))
    rhs = jnp.repeat(picked, freqs, axis=0)
    level = virt_energy[None, :] - shift[:, None]
    mag = level * level + DAMP * DAMP
    response = jnp.concatenate([rhs * level / mag, rhs * DAMP / mag], 0)
    den = shift[None, :, None] - offset[:, None, None] - virt_energy[None, None, :]
    den_mag = den * den + DAMP * DAMP
    own_rhs = lax.dynamic_slice_in_dim(rhs, mine * owned, owned)
    own_level = lax.dynamic_slice_in_dim(level, mine * owned, owned)
    own_mag = own_level * own_level + DAMP * DAMP
    own_re, own_im = own_rhs * own_level / own_mag, own_rhs * DAMP / own_mag
    slab = integral_slab.astype(F32)
    ampl = amplitudes.astype(F32)

    def dot(left, right, dims):
        return lax.dot_general(left, right, dims, precision=HIGHEST, preferred_element_type=F32)

    rms = []
    for sweep in range(ITERS):
        folded = dot(dot(response, slab, LAST), ampl, INNER)
        for slot in range(slots):
            inner = dot(response, coupling[slot], LAST)
            re, im = inner[:modes], inner[modes:]
            quot = jnp.concatenate(
                [
                    (re * den[slot] + im * DAMP) / den_mag[slot],
                    (im * den[slot] - re * DAMP) / den_mag[slot],
                ],
                0,
            )
            folded = folded + dot(quot, coupling[slot], INNER)
        pieces = folded.reshape(2, members, owned, virt).transpose(1, 0, 2, 3)
        total = jnp.sum(lax.all_to_all(pieces, group, 0, 0, tiled=True), 0)
        if not everyone:
            total = lax.psum(total, "narrow")
        res_re = own_rhs - (own_level * own_re + DAMP * own_im + total[0])
        res_im = -(own_level * own_im - DAMP * own_re + total[1])
        squares = jnp.sum(res_re * res_re + res_im * res_im, axis=1)
        rms.append(jnp.sqrt(squares / (2 * virt) + 1e-6))
        own_re = own_re + (res_re * own_level - res_im * DAMP) / own_mag
        own_im = own_im + (res_im * own_level + res_re * DAMP) / own_mag
        own = jnp.stack([own_re, own_im], 0)
        if sweep + 1 < ITERS:
            sent = jnp.broadcast_to(own[None], (members,) + own.shape)
            got = lax.all_to_all(sent, group, 0, 0, tiled=True)
            response = got.transpose(1, 0, 2, 3).reshape(2 * modes, virt)
    if everyone:
        sent = own.reshape(2, owned, narrow, block).transpose(2, 0, 1, 3)
        sent = jnp.broadcast_to(sent[None], (wide,) + sent.shape).reshape(members, 2, owned, block)
    else:
        sent = lax.dynamic_slice_in_dim(own, lax.axis_index("narrow") * block, block, 2)
        sent = jnp.broadcast_to(sent[None], (members,) + sent.shape)
    extra = jnp.broadcast_to(jnp.stack(rms, 0)[None, :, :, None], (members, 2, owned, LANE))
    got = lax.all_to_all(jnp.concatenate([sent, extra], 3), group, 0, 0, tiled=True)
    got = got.transpose(1, 0, 2, 3).reshape(2, modes, block + LANE)
    return got[:, :, :block], got[:, :, block]


def solution(mesh):
    wide, narrow = mesh.shape["wide"], mesh.shape["narrow"]
    chips = wide // 2
    finer = Mesh(mesh.devices.reshape(chips, 2, narrow), ("chip", "core", "narrow"))
    split = ("chip", "core", "narrow")

    def body(*args):
        virt, modes = args[5].shape[0], args[8].shape[0] * args[7].shape[0]
        pieces = (modes // SUB) * (virt // LANE)
        fits = (
            narrow == 2
            and pieces == 2 * chips * narrow
            and modes % (chips * narrow) == 0
            and SUB % (modes // (chips * narrow)) == 0
            and virt % (4 * LANE) == 0
        )
        if fits:
            return fast_path(chips, narrow, *args)
        return plain_path(wide, narrow, *args)

    return jax.shard_map(
        body,
        mesh=finer,
        in_specs=(
            P(split, None),
            P(split, None),
            P(split, None, None),
            P(),
            P(),
            P(),
            P(),
            P(),
            P(),
            P(None, "narrow"),
        ),
        out_specs=(P(None, None, "narrow"), P()),
        check_vma=False,
    )
```

```python
from functools import partial

import jax
import jax.numpy as jnp
from jax import lax
from jax.experimental import pallas as pl
from jax.experimental.pallas import tpu as pltpu
from jax.sharding import Mesh, PartitionSpec as P

ITERS = 2
DAMP = 0.5
HIGHEST = lax.Precision.HIGHEST
F32, BF16 = jnp.float32, jnp.bfloat16
LAST = (((1,), (1,)), ((), ()))
INNER = (((1,), (0,)), ((), ()))
SUB, LANE = 8, 128
VMEM = pl.BlockSpec(memory_space=pltpu.VMEM)
SMEM = pl.BlockSpec(memory_space=pltpu.SMEM)
HBM = pl.BlockSpec(memory_space=pltpu.HBM)
PARTS = 4
WINDOW = 6


def mxu(left, right, dims):
    return lax.dot_general(left, right, dims, preferred_element_type=F32)


def halves(value):
    high = value.astype(BF16)
    return high, (value - high.astype(F32)).astype(BF16)


def stacked(value):
    return jnp.concatenate(halves(value), 0)


def joined(value):
    rows = value.shape[0] // 2
    return value[:rows] + value[rows:]


def call(body, name, operands, in_specs, outs, scratch=(), flops=0, moved=0):
    operands = [
        pltpu.with_memory_space_constraint(x, pltpu.HBM) if spec is HBM else x
        for x, spec in zip(operands, in_specs)
    ]
    return pl.pallas_call(
        body,
        out_shape=[jax.ShapeDtypeStruct(s, d) for s, d in outs],
        in_specs=in_specs,
        out_specs=[VMEM] * len(outs),
        scratch_shapes=scratch,
        name=name,
        compiler_params=pltpu.CompilerParams(vmem_limit_bytes=20 << 20),
        cost_estimate=pl.CostEstimate(flops=flops, bytes_accessed=moved, transcendentals=0),
    )(*operands)


def start_all(pairs, sems):
    copies = [pltpu.make_async_copy(src, dst, sems.at[i]) for i, (src, dst) in enumerate(pairs)]
    for copy in copies:
        copy.start()
    return copies


def prepare_body(
    index_hbm,
    energy_hbm,
    frequency_hbm,
    blocks_hbm,
    pair_shift_hbm,
    virt_hbm,
    dipole_hbm,
    coupling_hbm,
    slab_hbm,
    picked,
    chosen,
    level,
    denom,
    high,
    low,
    slab_t,
    index,
    energy,
    frequency,
    blocks,
    pair_shift,
    virt,
    dipole,
    coupling,
    slab,
    small_sems,
    coupling_sems,
    slab_sems,
):
    freqs = frequency.shape[0]
    modes, columns = level.shape
    slots = coupling.shape[0]
    small = start_all(
        [
            (index_hbm, index),
            (energy_hbm, energy),
            (frequency_hbm, frequency),
            (blocks_hbm, blocks),
            (pair_shift_hbm, pair_shift),
            (virt_hbm, virt),
            (dipole_hbm, dipole),
        ],
        small_sems,
    )
    step = coupling.shape[1] // PARTS
    parts = [(s, slice(i * step, (i + 1) * step)) for s in range(slots) for i in range(PARTS)]
    coupled = [
        pltpu.make_async_copy(coupling_hbm.at[s, r], coupling.at[s, r], coupling_sems.at[i])
        for i, (s, r) in enumerate(parts)
    ]
    step = slab.shape[0] // PARTS
    pieces = [slice(i * step, (i + 1) * step) for i in range(PARTS)]
    slabs = [
        pltpu.make_async_copy(slab_hbm.at[r], slab.at[r], slab_sems.at[i])
        for i, r in enumerate(pieces)
    ]
    waiting = coupled + slabs

    def advance(count):
        for copy in waiting[:count]:
            copy.start()
        del waiting[:count]

    advance(WINDOW)
    for copy in small:
        copy.wait()
    orbital = lax.broadcasted_iota(jnp.int32, chosen.shape[1:], 0)
    for c in range(index.shape[0]):
        picked[c : c + 1] = dipole[pl.ds(index[c], 1)]
        chosen[c] = jnp.where(orbital == index[c], 1.0, 0.0)
    device = lax.axis_index(("chip", "core", "narrow"))
    rows = lax.broadcasted_iota(jnp.int32, (SUB, LANE), 0)
    tiles = []
    for start in range(0, modes, SUB):
        tile = jnp.zeros((SUB, LANE), F32)
        for k in range(start, start + SUB):
            value = frequency[k % freqs] + energy[index[k // freqs]]
            tile = jnp.where(rows == k - start, value, tile)
        tiles.append(tile)
    shift = jnp.concatenate(tiles, 0)
    for at in range(0, columns, LANE):
        here = jnp.broadcast_to(virt[:, at : at + LANE], (modes, LANE))
        level[:, at : at + LANE] = here - shift
        for s in range(slots):
            offset = pair_shift[blocks[device * slots + s]]
            denom[s, :, at : at + LANE] = (shift - offset) - here
    for (s, r), copy in zip(parts, coupled):
        copy.wait()
        advance(1)
        upper, lower = halves(coupling[s, r])
        high[s, r] = upper
        low[s, r] = lower
    for r, copy in zip(pieces, slabs):
        copy.wait()
        advance(1)
        slab_t[:, r] = slab[r].T


def fold(response, slab_t, high, low, dims):
    upper, lower = halves(response)
    both = jnp.concatenate([upper, lower], 0)
    singles = joined(mxu(both, slab_t, INNER))
    doubles = [joined(mxu(both, h, dims)) + mxu(upper, l, dims) for h, l in zip(high, low)]
    return singles, doubles


def quotient(inner, den):
    modes = den.shape[0]
    re, im = inner[:modes], inner[modes:]
    inverse = 1.0 / (den * den + DAMP * DAMP)
    return jnp.concatenate(
        [(re * den + im * DAMP) * inverse, (im * den - re * DAMP) * inverse], 0
    )


def unfold(singles, doubles, amplitudes, high, low, columns):
    total = mxu(singles[...], amplitudes[:, columns], INNER)
    slots, double = doubles.shape[:2]
    for s in range(slots):
        total = total + mxu(doubles[s], high[s, :, columns], INNER)
    total = joined(total)
    for s in range(slots):
        total = total + mxu(doubles[s, : double // 2], low[s, :, columns], INNER)
    return total


def write_tiles(out, total, modes):
    tiles = total.shape[1] // LANE
    for group in range(modes // SUB):
        for tile in range(tiles):
            piece, lanes = group * tiles + tile, slice(tile * LANE, (tile + 1) * LANE)
            out[piece, 0] = total[group * SUB : (group + 1) * SUB, lanes]
            out[piece, 1] = total[modes + group * SUB : modes + (group + 1) * SUB, lanes]


def first_body(
    own,
    other,
    chosen,
    level,
    denom,
    high,
    low,
    slab_t,
    amplitudes_hbm,
    rhs,
    start,
    singles,
    doubles,
    give,
    amplitudes,
    sems,
):
    step = amplitudes.shape[0] // PARTS
    copies = start_all(
        [
            (
                amplitudes_hbm.at[i * step : (i + 1) * step],
                amplitudes.at[i * step : (i + 1) * step],
            )
            for i in range(PARTS)
        ],
        sems,
    )
    modes, virt = level.shape
    cores, block = own.shape
    freqs = modes // cores
    side = lax.axis_index("narrow")
    here = pl.ds(pl.multiple_of(side * block, LANE), block)
    there = pl.ds(pl.multiple_of((1 - side) * block, LANE), block)
    for c in range(cores):
        span = slice(c * freqs, (c + 1) * freqs)
        mask = jnp.concatenate([chosen[c]] * (block // LANE), 1)
        theirs = jnp.sum(jnp.where(mask > 0.5, other[...], 0.0), axis=0, keepdims=True)
        rhs[span, here] = jnp.broadcast_to(own[c : c + 1], (freqs, block))
        rhs[span, there] = jnp.broadcast_to(theirs, (freqs, block))
    lev = level[...]
    inverse = 1.0 / (lev * lev + DAMP * DAMP)
    start[:modes] = rhs[...] * lev * inverse
    start[modes:] = rhs[...] * DAMP * inverse
    slots = range(high.shape[0])
    single, inner = fold(
        start[...], slab_t[...], [high[s] for s in slots], [low[s] for s in slots], LAST
    )
    singles[...] = stacked(single)
    for s, value in enumerate(inner):
        doubles[s] = stacked(quotient(value, denom[s]))
    for copy in copies:
        copy.wait()
    columns = pl.ds(pl.multiple_of((1 - lax.axis_index("core")) * (virt // 2), LANE), virt // 2)
    write_tiles(give, unfold(singles, doubles, amplitudes, high, low, columns), modes)


def first_rest_body(singles, doubles, amplitudes, high, low, keep, high_t, low_t):
    modes, half = singles.shape[0] // 4, high.shape[2] // 2
    core = lax.axis_index("core")
    columns = pl.ds(pl.multiple_of(core * half, LANE), half)
    rest = pl.ds(pl.multiple_of((1 - core) * half, LANE), half)
    write_tiles(keep, unfold(singles, doubles, amplitudes, high, low, columns), modes)
    for s in range(high.shape[0]):
        high_t[s] = high[s, :, rest].T
        low_t[s] = low[s, :, rest].T


def add_body(left, right, out):
    out[...] = left[...] + right[...]


def first_update_body(got, level, rhs, start, sent):
    members = got.shape[0]
    modes, virt = level.shape
    tiles = virt // 2 // LANE
    mine = lax.axis_index(("chip", "narrow"))
    group, tile = lax.div(mine, tiles), lax.rem(mine, tiles)
    column = lax.axis_index("core") * (virt // 2) + tile * LANE
    columns = pl.ds(pl.multiple_of(column, LANE), LANE)
    rows = pl.ds(pl.multiple_of(group * SUB, SUB), SUB)
    total = got[0]
    for j in range(1, members):
        total = total + got[j]
    lev, right = level[rows, columns], rhs[rows, columns]
    re = start[rows, columns]
    im = start[pl.ds(pl.multiple_of(modes + group * SUB, SUB), SUB), columns]
    inverse = 1.0 / (lev * lev + DAMP * DAMP)
    res_re = right - (lev * re + DAMP * im + total[0])
    res_im = -(lev * im - DAMP * re + total[1])
    re = re + (res_re * lev - res_im * DAMP) * inverse
    im = im + (res_im * lev + res_re * DAMP) * inverse
    for j in range(members):
        sent[j, 0] = re
        sent[j, 1] = im


def read_tiles(part, modes):
    tiles = part.shape[0] // (modes // SUB)
    rows = [
        jnp.concatenate([part[group * tiles + tile, q] for tile in range(tiles)], 1)
        for q in range(2)
        for group in range(modes // SUB)
    ]
    return jnp.concatenate(rows, 0)


def second_own_body(own, slab_t, high, low, response, singles, doubles):
    modes, half = response.shape[0] // 2, response.shape[1]
    mine = pl.ds(pl.multiple_of(lax.axis_index("core") * half, LANE), half)
    slots = range(high.shape[0])
    response[...] = read_tiles(own, modes)
    single, inner = fold(
        response[...],
        slab_t[mine],
        [high[s, :, mine] for s in slots],
        [low[s, :, mine] for s in slots],
        LAST,
    )
    singles[...] = single
    for s, value in enumerate(inner):
        doubles[s] = value


def write_owned(out, singles, doubles, amplitudes, high, low, at):
    members, double, half = out.shape
    owned, quarter = double // 2, half // 2
    modes = members * owned
    for side in range(2):
        columns = pl.ds(pl.multiple_of(side * half + at * quarter, LANE), quarter)
        total = unfold(singles, doubles, amplitudes, high, low, columns)
        lanes = slice(side * quarter, (side + 1) * quarter)
        for j in range(members):
            out[j, :owned, lanes] = total[j * owned : (j + 1) * owned]
            out[j, owned:, lanes] = total[modes + j * owned : modes + (j + 1) * owned]


def second_body(
    mine,
    other,
    single_part,
    double_part,
    denom,
    high,
    low,
    high_t,
    low_t,
    slab_t,
    amplitudes,
    response,
    singles,
    doubles,
    give,
):
    half = mine.shape[1]
    modes = mine.shape[0] // 2
    core = lax.axis_index("core")
    columns = pl.ds(pl.multiple_of(core * half, LANE), half)
    rest = pl.ds(pl.multiple_of((1 - core) * half, LANE), half)
    theirs = read_tiles(other, modes)
    response[:, columns] = mine[...]
    response[:, rest] = theirs
    slots = range(high_t.shape[0])
    single, inner = fold(
        theirs, slab_t[rest], [high_t[s] for s in slots], [low_t[s] for s in slots], INNER
    )
    singles[...] = stacked(single_part[...] + single)
    for s, value in enumerate(inner):
        doubles[s] = stacked(quotient(double_part[s] + value, denom[s]))
    write_owned(give, singles, doubles, amplitudes, high, low, 1 - core)


def second_rest_body(
    singles, doubles, amplitudes, high, low, level, start, response, keep, squares
):
    write_owned(keep, singles, doubles, amplitudes, high, low, lax.axis_index("core"))
    modes = level.shape[0]
    lev = level[...]
    re = response[:modes] - start[:modes]
    im = response[modes:] - start[modes:]
    res_re = lev * re + DAMP * im
    res_im = lev * im - DAMP * re
    squares[...] = jnp.sum(res_re * res_re + res_im * res_im, axis=1, keepdims=True)


def second_update_body(got, level, rhs, response, sent):
    members, double, width = got.shape
    owned = double // 2
    modes, virt = level.shape
    half, quarter = virt // 2, virt // 4
    mine = lax.axis_index(("chip", "narrow"))
    core = lax.axis_index("core")
    total = got[0]
    for j in range(1, members):
        total = total + got[j]
    per_tile = SUB // owned
    within = lax.rem(mine, per_tile)

    def own_rows(ref, first, columns):
        at = first + lax.div(mine, per_tile) * SUB
        tile = ref[pl.ds(pl.multiple_of(at, SUB), SUB), columns]
        rows = tile[:owned]
        for q in range(1, per_tile):
            rows = jnp.where(within == q, tile[q * owned : (q + 1) * owned], rows)
        return rows

    squares = jnp.zeros((owned, 1), F32)
    fresh = []
    for side in range(2):
        columns = pl.ds(pl.multiple_of(side * half + core * quarter, LANE), quarter)
        lanes = slice(side * quarter, (side + 1) * quarter)
        lev, right = own_rows(level, 0, columns), own_rows(rhs, 0, columns)
        re, im = own_rows(response, 0, columns), own_rows(response, modes, columns)
        inverse = 1.0 / (lev * lev + DAMP * DAMP)
        res_re = right - (lev * re + DAMP * im + total[:owned, lanes])
        res_im = -(lev * im - DAMP * re + total[owned:, lanes])
        squares += jnp.sum(res_re * res_re + res_im * res_im, axis=1, keepdims=True)
        re = re + (res_re * lev - res_im * DAMP) * inverse
        im = im + (res_im * lev + res_re * DAMP) * inverse
        fresh.append(jnp.concatenate([re, im], 0))
    lane = lax.broadcasted_iota(jnp.int32, (1, LANE), 1)
    tail = jnp.zeros((1, LANE), F32)
    for i in range(owned):
        tail = jnp.where(lane == i, jnp.broadcast_to(squares[i : i + 1], (1, LANE)), tail)
    for j in range(sent.shape[0]):
        for i in range(double):
            sent[j, :, i * quarter : (i + 1) * quarter] = fresh[j % 2][i : i + 1]
        sent[j, :, double * quarter :] = tail


def finish_body(got, old, response, rms):
    devices = got.shape[0]
    quarter = response.shape[2] // 2
    sweeps, modes = rms.shape
    owned = 2 * modes // devices
    double = 2 * owned
    row = lax.broadcasted_iota(jnp.int32, (sweeps, LANE), 0)
    lane = lax.broadcasted_iota(jnp.int32, (sweeps, LANE), 1)
    squares = jnp.zeros((sweeps, LANE), F32)
    for chip in range(devices // 4):
        for side in range(2):
            sources = [(chip * 2 + core) * 2 + side for core in range(2)]
            first = (chip * 2 + side) * owned
            for core, j in enumerate(sources):
                columns = slice(core * quarter, (core + 1) * quarter)
                for i in range(double):
                    k = first + i % owned
                    response[i // owned, k : k + 1, columns] = got[
                        j, :, i * quarter : (i + 1) * quarter
                    ]
            both = sum(got[j, :, double * quarter :] for j in sources)
            for i in range(owned):
                k = first + i
                value = jnp.broadcast_to(both[:, i : i + 1], (sweeps, LANE))
                squares = jnp.where((row == 1) & (lane == k), value, squares)
                value = jnp.broadcast_to(old[k : k + 1], (sweeps, LANE))
                squares = jnp.where((row == 0) & (lane == k), value, squares)
    virt = 4 * quarter
    rms[...] = jnp.sqrt(squares / (2 * virt) + 1e-6)[:, :modes]


def fast_path(
    chips,
    narrow,
    amplitudes,
    integral_slab,
    coupling,
    pair_of_block,
    pair_shift,
    virt_energy,
    core_energy,
    core_index,
    frequency,
    dipole,
):
    virt = virt_energy.shape[0]
    cores = core_index.shape[0]
    modes = frequency.shape[0] * cores
    slots = coupling.shape[0]
    block = dipole.shape[1]
    rows = amplitudes.shape[0]
    members = chips * narrow
    half = virt // 2
    flip_core = [(0, 1), (1, 0)]
    group = ("chip", "narrow")
    work = 8 * modes * virt * (virt * slots + rows)
    size = 2 * virt * (2 * virt * slots + rows)

    across = lax.ppermute(dipole, "narrow", flip_core)
    scalars = (core_index, core_energy, frequency, pair_of_block, pair_shift)
    picked, chosen, level, denom, high, low, slab_t = call(
        prepare_body,
        "prepare",
        scalars + (virt_energy[None], dipole, coupling, integral_slab),
        [HBM] * 9,
        [((cores, block), F32), ((cores, dipole.shape[0], LANE), F32)]
        + [((modes, virt), F32), ((slots, modes, virt), F32)]
        + [((slots, virt, virt), BF16)] * 2
        + [((virt, rows), BF16)],
        scratch=[pltpu.SMEM(a.shape, a.dtype) for a in scalars]
        + [
            pltpu.VMEM((1, virt), F32),
            pltpu.VMEM(dipole.shape, F32),
            pltpu.VMEM(coupling.shape, F32),
            pltpu.VMEM(integral_slab.shape, BF16),
            pltpu.SemaphoreType.DMA((7,)),
            pltpu.SemaphoreType.DMA((PARTS * slots,)),
            pltpu.SemaphoreType.DMA((PARTS,)),
        ],
        flops=4 * slots * virt * virt,
        moved=2 * size,
    )
    piece = (members, 2, SUB, LANE)
    between = [((4 * modes, rows), BF16), ((slots, 4 * modes, virt), BF16)]
    rhs, start, singles, doubles, give, held = call(
        first_body,
        "first",
        (picked, across, chosen, level, denom, high, low, slab_t, amplitudes),
        [VMEM] * 8 + [HBM],
        [((modes, virt), F32), ((2 * modes, virt), F32)]
        + between
        + [(piece, F32), (amplitudes.shape, BF16)],
        scratch=[pltpu.SemaphoreType.DMA((PARTS,))],
        flops=work * 3 // 4,
        moved=2 * size,
    )
    got = lax.ppermute(give, "core", flip_core)
    keep, high_t, low_t = call(
        first_rest_body,
        "first_rest",
        (singles, doubles, held, high, low),
        [VMEM] * 5,
        [(piece, F32)] + [((slots, half, virt), BF16)] * 2,
        flops=work // 4,
        moved=size // 2,
    )
    (total,) = call(add_body, "add_first", (keep, got), [VMEM] * 2, [(piece, F32)])
    got = lax.all_to_all(total, group, 0, 0, tiled=True)
    (sent,) = call(
        first_update_body, "first_update", (got, level, rhs, start), [VMEM] * 4, [(piece, F32)]
    )
    got = lax.all_to_all(sent, group, 0, 0, tiled=True)
    other = lax.ppermute(got, "core", flip_core)
    owned = modes // members
    piece = (members, 2 * owned, half)
    mine, single_part, double_part = call(
        second_own_body,
        "second_own",
        (got, slab_t, high, low),
        [VMEM] * 4,
        [
            ((2 * modes, half), F32),
            ((2 * modes, rows), F32),
            ((slots, 2 * modes, virt), F32),
        ],
        flops=work // 4,
        moved=size // 2,
    )
    response, singles, doubles, give = call(
        second_body,
        "second",
        (mine, other, single_part, double_part, denom, high, low, high_t, low_t, slab_t, held),
        [VMEM] * 11,
        [((2 * modes, virt), F32)] + between + [(piece, F32)],
        flops=work // 2,
        moved=size,
    )
    got = lax.ppermute(give, "core", flip_core)
    keep, old = call(
        second_rest_body,
        "second_rest",
        (singles, doubles, held, high, low, level, start, response),
        [VMEM] * 8,
        [(piece, F32), ((modes, 1), F32)],
        flops=work // 4,
        moved=size // 2,
    )
    (total,) = call(add_body, "add_second", (keep, got), [VMEM] * 2, [(piece, F32)])
    got = lax.all_to_all(total, group, 0, 0, tiled=True)
    piece = (2 * members, 1, owned * virt // 2 + LANE)
    (sent,) = call(
        second_update_body,
        "second_update",
        (got, level, rhs, response),
        [VMEM] * 4,
        [(piece, F32)],
    )
    got = lax.all_to_all(sent, ("chip", "core", "narrow"), 0, 0, tiled=True)
    return tuple(
        call(
            finish_body,
            "finish",
            (got, old),
            [VMEM] * 2,
            [((2, modes, block), F32), ((ITERS, modes), F32)],
        )
    )


def plain_path(
    wide,
    narrow,
    amplitudes,
    integral_slab,
    coupling,
    pair_of_block,
    pair_shift,
    virt_energy,
    core_energy,
    core_index,
    frequency,
    dipole,
):
    virt = virt_energy.shape[0]
    freqs = frequency.shape[0]
    modes = freqs * core_index.shape[0]
    slots = coupling.shape[0]
    block = dipole.shape[1]
    everyone = modes % (wide * narrow) == 0
    group = ("chip", "core", "narrow") if everyone else ("chip", "core")
    members = wide * narrow if everyone else wide
    owned = modes // members

    here = lax.axis_index(("chip", "core", "narrow"))
    mine = lax.axis_index(group)
    picked = jnp.take(dipole, core_index, axis=0)
    picked = lax.all_gather(picked, "narrow", axis=1, tiled=True)
    shift = (frequency[None, :] + jnp.take(core_energy, core_index)[:, None]).reshape(-1)
    offset = jnp.take(pair_shift, lax.dynamic_slice_in_dim(pair_of_block, here * slots, slots))
    rhs = jnp.repeat(picked, freqs, axis=0)
    level = virt_energy[None, :] - shift[:, None]
    mag = level * level + DAMP * DAMP
    response = jnp.concatenate([rhs * level / mag, rhs * DAMP / mag], 0)
    den = shift[None, :, None] - offset[:, None, None] - virt_energy[None, None, :]
    den_mag = den * den + DAMP * DAMP
    own_rhs = lax.dynamic_slice_in_dim(rhs, mine * owned, owned)
    own_level = lax.dynamic_slice_in_dim(level, mine * owned, owned)
    own_mag = own_level * own_level + DAMP * DAMP
    own_re, own_im = own_rhs * own_level / own_mag, own_rhs * DAMP / own_mag
    slab = integral_slab.astype(F32)
    ampl = amplitudes.astype(F32)

    def dot(left, right, dims):
        return lax.dot_general(left, right, dims, precision=HIGHEST, preferred_element_type=F32)

    rms = []
    for sweep in range(ITERS):
        folded = dot(dot(response, slab, LAST), ampl, INNER)
        for slot in range(slots):
            inner = dot(response, coupling[slot], LAST)
            re, im = inner[:modes], inner[modes:]
            quot = jnp.concatenate(
                [
                    (re * den[slot] + im * DAMP) / den_mag[slot],
                    (im * den[slot] - re * DAMP) / den_mag[slot],
                ],
                0,
            )
            folded = folded + dot(quot, coupling[slot], INNER)
        pieces = folded.reshape(2, members, owned, virt).transpose(1, 0, 2, 3)
        total = jnp.sum(lax.all_to_all(pieces, group, 0, 0, tiled=True), 0)
        if not everyone:
            total = lax.psum(total, "narrow")
        res_re = own_rhs - (own_level * own_re + DAMP * own_im + total[0])
        res_im = -(own_level * own_im - DAMP * own_re + total[1])
        squares = jnp.sum(res_re * res_re + res_im * res_im, axis=1)
        rms.append(jnp.sqrt(squares / (2 * virt) + 1e-6))
        own_re = own_re + (res_re * own_level - res_im * DAMP) / own_mag
        own_im = own_im + (res_im * own_level + res_re * DAMP) / own_mag
        own = jnp.stack([own_re, own_im], 0)
        if sweep + 1 < ITERS:
            sent = jnp.broadcast_to(own[None], (members,) + own.shape)
            got = lax.all_to_all(sent, group, 0, 0, tiled=True)
            response = got.transpose(1, 0, 2, 3).reshape(2 * modes, virt)
    if everyone:
        sent = own.reshape(2, owned, narrow, block).transpose(2, 0, 1, 3)
        sent = jnp.broadcast_to(sent[None], (wide,) + sent.shape).reshape(members, 2, owned, block)
    else:
        sent = lax.dynamic_slice_in_dim(own, lax.axis_index("narrow") * block, block, 2)
        sent = jnp.broadcast_to(sent[None], (members,) + sent.shape)
    extra = jnp.broadcast_to(jnp.stack(rms, 0)[None, :, :, None], (members, 2, owned, LANE))
    got = lax.all_to_all(jnp.concatenate([sent, extra], 3), group, 0, 0, tiled=True)
    got = got.transpose(1, 0, 2, 3).reshape(2, modes, block + LANE)
    return got[:, :, :block], got[:, :, block]


def solution(mesh):
    wide, narrow = mesh.shape["wide"], mesh.shape["narrow"]
    chips = wide // 2
    finer = Mesh(mesh.devices.reshape(chips, 2, narrow), ("chip", "core", "narrow"))
    split = ("chip", "core", "narrow")

    def body(*args):
        virt, modes = args[5].shape[0], args[8].shape[0] * args[7].shape[0]
        pieces = (modes // SUB) * (virt // LANE)
        fits = (
            narrow == 2
            and pieces == 2 * chips * narrow
            and modes % (chips * narrow) == 0
            and SUB % (modes // (chips * narrow)) == 0
            and virt % (4 * LANE) == 0
        )
        if fits:
            return fast_path(chips, narrow, *args)
        return plain_path(wide, narrow, *args)

    return jax.shard_map(
        body,
        mesh=finer,
        in_specs=(
            P(split, None),
            P(split, None),
            P(split, None, None),
            P(),
            P(),
            P(),
            P(),
            P(),
            P(),
            P(None, "narrow"),
        ),
        out_specs=(P(None, None, "narrow"), P()),
        check_vma=False,
    )
```

```python
from functools import partial

import jax
import jax.numpy as jnp
from jax import lax
from jax.experimental import pallas as pl
from jax.experimental.pallas import tpu as pltpu
from jax.sharding import Mesh, PartitionSpec as P

ITERS = 2
DAMP = 0.5
HIGHEST = lax.Precision.HIGHEST
F32, BF16 = jnp.float32, jnp.bfloat16
LAST = (((1,), (1,)), ((), ()))
INNER = (((1,), (0,)), ((), ()))
SUB, LANE = 8, 128
VMEM = pl.BlockSpec(memory_space=pltpu.VMEM)
SMEM = pl.BlockSpec(memory_space=pltpu.SMEM)
HBM = pl.BlockSpec(memory_space=pltpu.HBM)
PARTS = 4
WINDOW = 6


def mxu(left, right, dims):
    return lax.dot_general(left, right, dims, preferred_element_type=F32)


def halves(value):
    high = value.astype(BF16)
    return high, (value - high.astype(F32)).astype(BF16)


def stacked(value):
    return jnp.concatenate(halves(value), 0)


def joined(value):
    rows = value.shape[0] // 2
    return value[:rows] + value[rows:]


def call(body, name, operands, in_specs, outs, scratch=(), flops=0, moved=0):
    operands = [
        pltpu.with_memory_space_constraint(x, pltpu.HBM) if spec is HBM else x
        for x, spec in zip(operands, in_specs)
    ]
    return pl.pallas_call(
        body,
        out_shape=[jax.ShapeDtypeStruct(s, d) for s, d in outs],
        in_specs=in_specs,
        out_specs=[VMEM] * len(outs),
        scratch_shapes=scratch,
        name=name,
        compiler_params=pltpu.CompilerParams(vmem_limit_bytes=20 << 20),
        cost_estimate=pl.CostEstimate(flops=flops, bytes_accessed=moved, transcendentals=0),
    )(*operands)


def start_all(pairs, sems):
    copies = [pltpu.make_async_copy(src, dst, sems.at[i]) for i, (src, dst) in enumerate(pairs)]
    for copy in copies:
        copy.start()
    return copies


def prepare_body(
    index_hbm,
    energy_hbm,
    frequency_hbm,
    blocks_hbm,
    pair_shift_hbm,
    virt_hbm,
    dipole_hbm,
    coupling_hbm,
    slab_hbm,
    picked,
    chosen,
    level,
    denom,
    high,
    low,
    slab_t,
    index,
    energy,
    frequency,
    blocks,
    pair_shift,
    virt,
    dipole,
    coupling,
    slab,
    small_sems,
    coupling_sems,
    slab_sems,
):
    freqs = frequency.shape[0]
    modes, columns = level.shape
    slots = coupling.shape[0]
    small = start_all(
        [
            (index_hbm, index),
            (energy_hbm, energy),
            (frequency_hbm, frequency),
            (blocks_hbm, blocks),
            (pair_shift_hbm, pair_shift),
            (virt_hbm, virt),
            (dipole_hbm, dipole),
        ],
        small_sems,
    )
    step = coupling.shape[1] // PARTS
    parts = [(s, slice(i * step, (i + 1) * step)) for s in range(slots) for i in range(PARTS)]
    coupled = [
        pltpu.make_async_copy(coupling_hbm.at[s, r], coupling.at[s, r], coupling_sems.at[i])
        for i, (s, r) in enumerate(parts)
    ]
    step = slab.shape[0] // PARTS
    pieces = [slice(i * step, (i + 1) * step) for i in range(PARTS)]
    slabs = [
        pltpu.make_async_copy(slab_hbm.at[r], slab.at[r], slab_sems.at[i])
        for i, r in enumerate(pieces)
    ]
    waiting = coupled + slabs

    def advance(count):
        for copy in waiting[:count]:
            copy.start()
        del waiting[:count]

    advance(WINDOW)
    for copy in small:
        copy.wait()
    orbital = lax.broadcasted_iota(jnp.int32, chosen.shape[1:], 0)
    for c in range(index.shape[0]):
        picked[c : c + 1] = dipole[pl.ds(index[c], 1)]
        chosen[c] = jnp.where(orbital == index[c], 1.0, 0.0)
    device = lax.axis_index(("chip", "core", "narrow"))
    rows = lax.broadcasted_iota(jnp.int32, (SUB, LANE), 0)
    tiles = []
    for start in range(0, modes, SUB):
        tile = jnp.zeros((SUB, LANE), F32)
        for k in range(start, start + SUB):
            value = frequency[k % freqs] + energy[index[k // freqs]]
            tile = jnp.where(rows == k - start, value, tile)
        tiles.append(tile)
    shift = jnp.concatenate(tiles, 0)
    for at in range(0, columns, LANE):
        here = jnp.broadcast_to(virt[:, at : at + LANE], (modes, LANE))
        level[:, at : at + LANE] = here - shift
        for s in range(slots):
            offset = pair_shift[blocks[device * slots + s]]
            denom[s, :, at : at + LANE] = (shift - offset) - here
    for (s, r), copy in zip(parts, coupled):
        copy.wait()
        advance(1)
        upper, lower = halves(coupling[s, r])
        high[s, r] = upper
        low[s, r] = lower
    for r, copy in zip(pieces, slabs):
        copy.wait()
        advance(1)
        slab_t[:, r] = slab[r].T


def fold(response, slab_t, high, low, dims):
    upper, lower = halves(response)
    both = jnp.concatenate([upper, lower], 0)
    singles = joined(mxu(both, slab_t, INNER))
    doubles = [joined(mxu(both, h, dims)) + mxu(upper, l, dims) for h, l in zip(high, low)]
    return singles, doubles


def quotient(inner, den):
    modes = den.shape[0]
    re, im = inner[:modes], inner[modes:]
    inverse = 1.0 / (den * den + DAMP * DAMP)
    return jnp.concatenate(
        [(re * den + im * DAMP) * inverse, (im * den - re * DAMP) * inverse], 0
    )


def unfold(singles, doubles, amplitudes, high, low, columns):
    total = mxu(singles[...], amplitudes[:, columns], INNER)
    slots, double = doubles.shape[:2]
    for s in range(slots):
        total = total + mxu(doubles[s], high[s, :, columns], INNER)
    total = joined(total)
    for s in range(slots):
        total = total + mxu(doubles[s, : double // 2], low[s, :, columns], INNER)
    return total


def write_tiles(out, total, modes):
    tiles = total.shape[1] // LANE
    for group in range(modes // SUB):
        for tile in range(tiles):
            piece, lanes = group * tiles + tile, slice(tile * LANE, (tile + 1) * LANE)
            out[piece, 0] = total[group * SUB : (group + 1) * SUB, lanes]
            out[piece, 1] = total[modes + group * SUB : modes + (group + 1) * SUB, lanes]


def first_body(
    own,
    other,
    chosen,
    level,
    denom,
    high,
    low,
    slab_t,
    amplitudes,
    rhs,
    start,
    singles,
    doubles,
    give,
):
    modes, virt = level.shape
    cores, block = own.shape
    freqs = modes // cores
    side = lax.axis_index("narrow")
    here = pl.ds(pl.multiple_of(side * block, LANE), block)
    there = pl.ds(pl.multiple_of((1 - side) * block, LANE), block)
    for c in range(cores):
        span = slice(c * freqs, (c + 1) * freqs)
        mask = jnp.concatenate([chosen[c]] * (block // LANE), 1)
        theirs = jnp.sum(jnp.where(mask > 0.5, other[...], 0.0), axis=0, keepdims=True)
        rhs[span, here] = jnp.broadcast_to(own[c : c + 1], (freqs, block))
        rhs[span, there] = jnp.broadcast_to(theirs, (freqs, block))
    lev = level[...]
    inverse = 1.0 / (lev * lev + DAMP * DAMP)
    start[:modes] = rhs[...] * lev * inverse
    start[modes:] = rhs[...] * DAMP * inverse
    slots = range(high.shape[0])
    single, inner = fold(
        start[...], slab_t[...], [high[s] for s in slots], [low[s] for s in slots], LAST
    )
    singles[...] = stacked(single)
    for s, value in enumerate(inner):
        doubles[s] = stacked(quotient(value, denom[s]))
    columns = pl.ds(pl.multiple_of((1 - lax.axis_index("core")) * (virt // 2), LANE), virt // 2)
    write_tiles(give, unfold(singles, doubles, amplitudes, high, low, columns), modes)


def first_rest_body(singles, doubles, amplitudes, high, low, keep, high_t, low_t):
    modes, half = singles.shape[0] // 4, high.shape[2] // 2
    core = lax.axis_index("core")
    columns = pl.ds(pl.multiple_of(core * half, LANE), half)
    rest = pl.ds(pl.multiple_of((1 - core) * half, LANE), half)
    write_tiles(keep, unfold(singles, doubles, amplitudes, high, low, columns), modes)
    for s in range(high.shape[0]):
        high_t[s] = high[s, :, rest].T
        low_t[s] = low[s, :, rest].T


def add_body(left, right, out):
    out[...] = left[...] + right[...]


def first_update_body(got, level, rhs, start, sent):
    members = got.shape[0]
    modes, virt = level.shape
    tiles = virt // 2 // LANE
    mine = lax.axis_index(("chip", "narrow"))
    group, tile = lax.div(mine, tiles), lax.rem(mine, tiles)
    column = lax.axis_index("core") * (virt // 2) + tile * LANE
    columns = pl.ds(pl.multiple_of(column, LANE), LANE)
    rows = pl.ds(pl.multiple_of(group * SUB, SUB), SUB)
    total = got[0]
    for j in range(1, members):
        total = total + got[j]
    lev, right = level[rows, columns], rhs[rows, columns]
    re = start[rows, columns]
    im = start[pl.ds(pl.multiple_of(modes + group * SUB, SUB), SUB), columns]
    inverse = 1.0 / (lev * lev + DAMP * DAMP)
    res_re = right - (lev * re + DAMP * im + total[0])
    res_im = -(lev * im - DAMP * re + total[1])
    re = re + (res_re * lev - res_im * DAMP) * inverse
    im = im + (res_im * lev + res_re * DAMP) * inverse
    for j in range(members):
        sent[j, 0] = re
        sent[j, 1] = im


def read_tiles(part, modes):
    tiles = part.shape[0] // (modes // SUB)
    rows = [
        jnp.concatenate([part[group * tiles + tile, q] for tile in range(tiles)], 1)
        for q in range(2)
        for group in range(modes // SUB)
    ]
    return jnp.concatenate(rows, 0)


def second_own_body(own, slab_t, high, low, response, singles, doubles):
    modes, half = response.shape[0] // 2, response.shape[1]
    mine = pl.ds(pl.multiple_of(lax.axis_index("core") * half, LANE), half)
    slots = range(high.shape[0])
    response[...] = read_tiles(own, modes)
    single, inner = fold(
        response[...],
        slab_t[mine],
        [high[s, :, mine] for s in slots],
        [low[s, :, mine] for s in slots],
        LAST,
    )
    singles[...] = single
    for s, value in enumerate(inner):
        doubles[s] = value


def write_owned(out, singles, doubles, amplitudes, high, low, at):
    members, double, half = out.shape
    owned, quarter = double // 2, half // 2
    modes = members * owned
    for side in range(2):
        columns = pl.ds(pl.multiple_of(side * half + at * quarter, LANE), quarter)
        total = unfold(singles, doubles, amplitudes, high, low, columns)
        lanes = slice(side * quarter, (side + 1) * quarter)
        for j in range(members):
            out[j, :owned, lanes] = total[j * owned : (j + 1) * owned]
            out[j, owned:, lanes] = total[modes + j * owned : modes + (j + 1) * owned]


def second_body(
    mine,
    other,
    single_part,
    double_part,
    denom,
    high,
    low,
    high_t,
    low_t,
    slab_t,
    amplitudes,
    response,
    singles,
    doubles,
    give,
):
    half = mine.shape[1]
    modes = mine.shape[0] // 2
    core = lax.axis_index("core")
    columns = pl.ds(pl.multiple_of(core * half, LANE), half)
    rest = pl.ds(pl.multiple_of((1 - core) * half, LANE), half)
    theirs = read_tiles(other, modes)
    response[:, columns] = mine[...]
    response[:, rest] = theirs
    slots = range(high_t.shape[0])
    single, inner = fold(
        theirs, slab_t[rest], [high_t[s] for s in slots], [low_t[s] for s in slots], INNER
    )
    singles[...] = stacked(single_part[...] + single)
    for s, value in enumerate(inner):
        doubles[s] = stacked(quotient(double_part[s] + value, denom[s]))
    write_owned(give, singles, doubles, amplitudes, high, low, 1 - core)


def second_rest_body(
    singles, doubles, amplitudes, high, low, level, start, response, keep, squares
):
    write_owned(keep, singles, doubles, amplitudes, high, low, lax.axis_index("core"))
    modes = level.shape[0]
    lev = level[...]
    re = response[:modes] - start[:modes]
    im = response[modes:] - start[modes:]
    res_re = lev * re + DAMP * im
    res_im = lev * im - DAMP * re
    squares[...] = jnp.sum(res_re * res_re + res_im * res_im, axis=1, keepdims=True)


def second_update_body(got, level, rhs, response, sent):
    members, double, width = got.shape
    owned = double // 2
    modes, virt = level.shape
    half, quarter = virt // 2, virt // 4
    mine = lax.axis_index(("chip", "narrow"))
    core = lax.axis_index("core")
    total = got[0]
    for j in range(1, members):
        total = total + got[j]
    per_tile = SUB // owned
    within = lax.rem(mine, per_tile)

    def own_rows(ref, first, columns):
        at = first + lax.div(mine, per_tile) * SUB
        tile = ref[pl.ds(pl.multiple_of(at, SUB), SUB), columns]
        rows = tile[:owned]
        for q in range(1, per_tile):
            rows = jnp.where(within == q, tile[q * owned : (q + 1) * owned], rows)
        return rows

    squares = jnp.zeros((owned, 1), F32)
    fresh = []
    for side in range(2):
        columns = pl.ds(pl.multiple_of(side * half + core * quarter, LANE), quarter)
        lanes = slice(side * quarter, (side + 1) * quarter)
        lev, right = own_rows(level, 0, columns), own_rows(rhs, 0, columns)
        re, im = own_rows(response, 0, columns), own_rows(response, modes, columns)
        inverse = 1.0 / (lev * lev + DAMP * DAMP)
        res_re = right - (lev * re + DAMP * im + total[:owned, lanes])
        res_im = -(lev * im - DAMP * re + total[owned:, lanes])
        squares += jnp.sum(res_re * res_re + res_im * res_im, axis=1, keepdims=True)
        re = re + (res_re * lev - res_im * DAMP) * inverse
        im = im + (res_im * lev + res_re * DAMP) * inverse
        fresh.append(jnp.concatenate([re, im], 0))
    lane = lax.broadcasted_iota(jnp.int32, (1, LANE), 1)
    tail = jnp.zeros((1, LANE), F32)
    for i in range(owned):
        tail = jnp.where(lane == i, jnp.broadcast_to(squares[i : i + 1], (1, LANE)), tail)
    for j in range(sent.shape[0]):
        for i in range(double):
            sent[j, :, i * quarter : (i + 1) * quarter] = fresh[j % 2][i : i + 1]
        sent[j, :, double * quarter :] = tail


def finish_body(got, old, response, rms):
    devices = got.shape[0]
    quarter = response.shape[2] // 2
    sweeps, modes = rms.shape
    owned = 2 * modes // devices
    double = 2 * owned
    row = lax.broadcasted_iota(jnp.int32, (sweeps, LANE), 0)
    lane = lax.broadcasted_iota(jnp.int32, (sweeps, LANE), 1)
    squares = jnp.zeros((sweeps, LANE), F32)
    for chip in range(devices // 4):
        for side in range(2):
            sources = [(chip * 2 + core) * 2 + side for core in range(2)]
            first = (chip * 2 + side) * owned
            for core, j in enumerate(sources):
                columns = slice(core * quarter, (core + 1) * quarter)
                for i in range(double):
                    k = first + i % owned
                    response[i // owned, k : k + 1, columns] = got[
                        j, :, i * quarter : (i + 1) * quarter
                    ]
            both = sum(got[j, :, double * quarter :] for j in sources)
            for i in range(owned):
                k = first + i
                value = jnp.broadcast_to(both[:, i : i + 1], (sweeps, LANE))
                squares = jnp.where((row == 1) & (lane == k), value, squares)
                value = jnp.broadcast_to(old[k : k + 1], (sweeps, LANE))
                squares = jnp.where((row == 0) & (lane == k), value, squares)
    virt = 4 * quarter
    rms[...] = jnp.sqrt(squares / (2 * virt) + 1e-6)[:, :modes]


def fast_path(
    chips,
    narrow,
    amplitudes,
    integral_slab,
    coupling,
    pair_of_block,
    pair_shift,
    virt_energy,
    core_energy,
    core_index,
    frequency,
    dipole,
):
    virt = virt_energy.shape[0]
    cores = core_index.shape[0]
    modes = frequency.shape[0] * cores
    slots = coupling.shape[0]
    block = dipole.shape[1]
    rows = amplitudes.shape[0]
    members = chips * narrow
    half = virt // 2
    flip_core = [(0, 1), (1, 0)]
    group = ("chip", "narrow")
    work = 8 * modes * virt * (virt * slots + rows)
    size = 2 * virt * (2 * virt * slots + rows)

    across = lax.ppermute(dipole, "narrow", flip_core)
    scalars = (core_index, core_energy, frequency, pair_of_block, pair_shift)
    picked, chosen, level, denom, high, low, slab_t = call(
        prepare_body,
        "prepare",
        scalars + (virt_energy[None], dipole, coupling, integral_slab),
        [HBM] * 9,
        [((cores, block), F32), ((cores, dipole.shape[0], LANE), F32)]
        + [((modes, virt), F32), ((slots, modes, virt), F32)]
        + [((slots, virt, virt), BF16)] * 2
        + [((virt, rows), BF16)],
        scratch=[pltpu.SMEM(a.shape, a.dtype) for a in scalars]
        + [
            pltpu.VMEM((1, virt), F32),
            pltpu.VMEM(dipole.shape, F32),
            pltpu.VMEM(coupling.shape, F32),
            pltpu.VMEM(integral_slab.shape, BF16),
            pltpu.SemaphoreType.DMA((7,)),
            pltpu.SemaphoreType.DMA((PARTS * slots,)),
            pltpu.SemaphoreType.DMA((PARTS,)),
        ],
        flops=4 * slots * virt * virt,
        moved=2 * size,
    )
    piece = (members, 2, SUB, LANE)
    between = [((4 * modes, rows), BF16), ((slots, 4 * modes, virt), BF16)]
    rhs, start, singles, doubles, give = call(
        first_body,
        "first",
        (picked, across, chosen, level, denom, high, low, slab_t, amplitudes),
        [VMEM] * 9,
        [((modes, virt), F32), ((2 * modes, virt), F32)]
        + between
        + [(piece, F32)],
        flops=work * 3 // 4,
        moved=2 * size,
    )
    got = lax.ppermute(give, "core", flip_core)
    keep, high_t, low_t = call(
        first_rest_body,
        "first_rest",
        (singles, doubles, amplitudes, high, low),
        [VMEM] * 5,
        [(piece, F32)] + [((slots, half, virt), BF16)] * 2,
        flops=work // 4,
        moved=size // 2,
    )
    (total,) = call(add_body, "add_first", (keep, got), [VMEM] * 2, [(piece, F32)])
    got = lax.all_to_all(total, group, 0, 0, tiled=True)
    (sent,) = call(
        first_update_body, "first_update", (got, level, rhs, start), [VMEM] * 4, [(piece, F32)]
    )
    got = lax.all_to_all(sent, group, 0, 0, tiled=True)
    other = lax.ppermute(got, "core", flip_core)
    owned = modes // members
    piece = (members, 2 * owned, half)
    mine, single_part, double_part = call(
        second_own_body,
        "second_own",
        (got, slab_t, high, low),
        [VMEM] * 4,
        [
            ((2 * modes, half), F32),
            ((2 * modes, rows), F32),
            ((slots, 2 * modes, virt), F32),
        ],
        flops=work // 4,
        moved=size // 2,
    )
    response, singles, doubles, give = call(
        second_body,
        "second",
        (mine, other, single_part, double_part, denom, high, low, high_t, low_t, slab_t, amplitudes),
        [VMEM] * 11,
        [((2 * modes, virt), F32)] + between + [(piece, F32)],
        flops=work // 2,
        moved=size,
    )
    got = lax.ppermute(give, "core", flip_core)
    keep, old = call(
        second_rest_body,
        "second_rest",
        (singles, doubles, amplitudes, high, low, level, start, response),
        [VMEM] * 8,
        [(piece, F32), ((modes, 1), F32)],
        flops=work // 4,
        moved=size // 2,
    )
    (total,) = call(add_body, "add_second", (keep, got), [VMEM] * 2, [(piece, F32)])
    got = lax.all_to_all(total, group, 0, 0, tiled=True)
    piece = (2 * members, 1, owned * virt // 2 + LANE)
    (sent,) = call(
        second_update_body,
        "second_update",
        (got, level, rhs, response),
        [VMEM] * 4,
        [(piece, F32)],
    )
    got = lax.all_to_all(sent, ("chip", "core", "narrow"), 0, 0, tiled=True)
    return tuple(
        call(
            finish_body,
            "finish",
            (got, old),
            [VMEM] * 2,
            [((2, modes, block), F32), ((ITERS, modes), F32)],
        )
    )


def plain_path(
    wide,
    narrow,
    amplitudes,
    integral_slab,
    coupling,
    pair_of_block,
    pair_shift,
    virt_energy,
    core_energy,
    core_index,
    frequency,
    dipole,
):
    virt = virt_energy.shape[0]
    freqs = frequency.shape[0]
    modes = freqs * core_index.shape[0]
    slots = coupling.shape[0]
    block = dipole.shape[1]
    everyone = modes % (wide * narrow) == 0
    group = ("chip", "core", "narrow") if everyone else ("chip", "core")
    members = wide * narrow if everyone else wide
    owned = modes // members

    here = lax.axis_index(("chip", "core", "narrow"))
    mine = lax.axis_index(group)
    picked = jnp.take(dipole, core_index, axis=0)
    picked = lax.all_gather(picked, "narrow", axis=1, tiled=True)
    shift = (frequency[None, :] + jnp.take(core_energy, core_index)[:, None]).reshape(-1)
    offset = jnp.take(pair_shift, lax.dynamic_slice_in_dim(pair_of_block, here * slots, slots))
    rhs = jnp.repeat(picked, freqs, axis=0)
    level = virt_energy[None, :] - shift[:, None]
    mag = level * level + DAMP * DAMP
    response = jnp.concatenate([rhs * level / mag, rhs * DAMP / mag], 0)
    den = shift[None, :, None] - offset[:, None, None] - virt_energy[None, None, :]
    den_mag = den * den + DAMP * DAMP
    own_rhs = lax.dynamic_slice_in_dim(rhs, mine * owned, owned)
    own_level = lax.dynamic_slice_in_dim(level, mine * owned, owned)
    own_mag = own_level * own_level + DAMP * DAMP
    own_re, own_im = own_rhs * own_level / own_mag, own_rhs * DAMP / own_mag
    slab = integral_slab.astype(F32)
    ampl = amplitudes.astype(F32)

    def dot(left, right, dims):
        return lax.dot_general(left, right, dims, precision=HIGHEST, preferred_element_type=F32)

    rms = []
    for sweep in range(ITERS):
        folded = dot(dot(response, slab, LAST), ampl, INNER)
        for slot in range(slots):
            inner = dot(response, coupling[slot], LAST)
            re, im = inner[:modes], inner[modes:]
            quot = jnp.concatenate(
                [
                    (re * den[slot] + im * DAMP) / den_mag[slot],
                    (im * den[slot] - re * DAMP) / den_mag[slot],
                ],
                0,
            )
            folded = folded + dot(quot, coupling[slot], INNER)
        pieces = folded.reshape(2, members, owned, virt).transpose(1, 0, 2, 3)
        total = jnp.sum(lax.all_to_all(pieces, group, 0, 0, tiled=True), 0)
        if not everyone:
            total = lax.psum(total, "narrow")
        res_re = own_rhs - (own_level * own_re + DAMP * own_im + total[0])
        res_im = -(own_level * own_im - DAMP * own_re + total[1])
        squares = jnp.sum(res_re * res_re + res_im * res_im, axis=1)
        rms.append(jnp.sqrt(squares / (2 * virt) + 1e-6))
        own_re = own_re + (res_re * own_level - res_im * DAMP) / own_mag
        own_im = own_im + (res_im * own_level + res_re * DAMP) / own_mag
        own = jnp.stack([own_re, own_im], 0)
        if sweep + 1 < ITERS:
            sent = jnp.broadcast_to(own[None], (members,) + own.shape)
            got = lax.all_to_all(sent, group, 0, 0, tiled=True)
            response = got.transpose(1, 0, 2, 3).reshape(2 * modes, virt)
    if everyone:
        sent = own.reshape(2, owned, narrow, block).transpose(2, 0, 1, 3)
        sent = jnp.broadcast_to(sent[None], (wide,) + sent.shape).reshape(members, 2, owned, block)
    else:
        sent = lax.dynamic_slice_in_dim(own, lax.axis_index("narrow") * block, block, 2)
        sent = jnp.broadcast_to(sent[None], (members,) + sent.shape)
    extra = jnp.broadcast_to(jnp.stack(rms, 0)[None, :, :, None], (members, 2, owned, LANE))
    got = lax.all_to_all(jnp.concatenate([sent, extra], 3), group, 0, 0, tiled=True)
    got = got.transpose(1, 0, 2, 3).reshape(2, modes, block + LANE)
    return got[:, :, :block], got[:, :, block]


def solution(mesh):
    wide, narrow = mesh.shape["wide"], mesh.shape["narrow"]
    chips = wide // 2
    finer = Mesh(mesh.devices.reshape(chips, 2, narrow), ("chip", "core", "narrow"))
    split = ("chip", "core", "narrow")

    def body(*args):
        virt, modes = args[5].shape[0], args[8].shape[0] * args[7].shape[0]
        pieces = (modes // SUB) * (virt // LANE)
        fits = (
            narrow == 2
            and pieces == 2 * chips * narrow
            and modes % (chips * narrow) == 0
            and SUB % (modes // (chips * narrow)) == 0
            and virt % (4 * LANE) == 0
        )
        if fits:
            return fast_path(chips, narrow, *args)
        return plain_path(wide, narrow, *args)

    return jax.shard_map(
        body,
        mesh=finer,
        in_specs=(
            P(split, None),
            P(split, None),
            P(split, None, None),
            P(),
            P(),
            P(),
            P(),
            P(),
            P(),
            P(None, "narrow"),
        ),
        out_specs=(P(None, None, "narrow"), P()),
        check_vma=False,
    )
```

```python
from functools import partial

import jax
import jax.numpy as jnp
from jax import lax
from jax.experimental import pallas as pl
from jax.experimental.pallas import tpu as pltpu
from jax.sharding import Mesh, PartitionSpec as P

ITERS = 2
DAMP = 0.5
HIGHEST = lax.Precision.HIGHEST
F32, BF16 = jnp.float32, jnp.bfloat16
LAST = (((1,), (1,)), ((), ()))
INNER = (((1,), (0,)), ((), ()))
SUB, LANE = 8, 128
VMEM = pl.BlockSpec(memory_space=pltpu.VMEM)
SMEM = pl.BlockSpec(memory_space=pltpu.SMEM)
HBM = pl.BlockSpec(memory_space=pltpu.HBM)
PARTS = 4
WINDOW = 6


def mxu(left, right, dims):
    return lax.dot_general(left, right, dims, preferred_element_type=F32)


def halves(value):
    high = value.astype(BF16)
    return high, (value - high.astype(F32)).astype(BF16)


def stacked(value):
    return jnp.concatenate(halves(value), 0)


def joined(value):
    rows = value.shape[0] // 2
    return value[:rows] + value[rows:]


def call(body, name, operands, in_specs, outs, scratch=(), flops=0, moved=0):
    operands = [
        pltpu.with_memory_space_constraint(x, pltpu.HBM) if spec is HBM else x
        for x, spec in zip(operands, in_specs)
    ]
    return pl.pallas_call(
        body,
        out_shape=[jax.ShapeDtypeStruct(s, d) for s, d in outs],
        in_specs=in_specs,
        out_specs=[VMEM] * len(outs),
        scratch_shapes=scratch,
        name=name,
        compiler_params=pltpu.CompilerParams(vmem_limit_bytes=20 << 20),
        cost_estimate=pl.CostEstimate(flops=flops, bytes_accessed=moved, transcendentals=0),
    )(*operands)


def start_all(pairs, sems):
    copies = [pltpu.make_async_copy(src, dst, sems.at[i]) for i, (src, dst) in enumerate(pairs)]
    for copy in copies:
        copy.start()
    return copies


def prepare_body(
    index_hbm,
    energy_hbm,
    frequency_hbm,
    blocks_hbm,
    pair_shift_hbm,
    virt_hbm,
    dipole_hbm,
    coupling_hbm,
    picked,
    chosen,
    level,
    denom,
    high,
    low,
    index,
    energy,
    frequency,
    blocks,
    pair_shift,
    virt,
    dipole,
    coupling,
    small_sems,
    coupling_sems,
):
    freqs = frequency.shape[0]
    modes, columns = level.shape
    slots = coupling.shape[0]
    small = start_all(
        [
            (index_hbm, index),
            (energy_hbm, energy),
            (frequency_hbm, frequency),
            (blocks_hbm, blocks),
            (pair_shift_hbm, pair_shift),
            (virt_hbm, virt),
            (dipole_hbm, dipole),
        ],
        small_sems,
    )
    step = coupling.shape[1] // PARTS
    parts = [(s, slice(i * step, (i + 1) * step)) for s in range(slots) for i in range(PARTS)]
    coupled = [
        pltpu.make_async_copy(coupling_hbm.at[s, r], coupling.at[s, r], coupling_sems.at[i])
        for i, (s, r) in enumerate(parts)
    ]
    waiting = list(coupled)

    def advance(count):
        for copy in waiting[:count]:
            copy.start()
        del waiting[:count]

    advance(WINDOW)
    for copy in small:
        copy.wait()
    orbital = lax.broadcasted_iota(jnp.int32, chosen.shape[1:], 0)
    for c in range(index.shape[0]):
        picked[c : c + 1] = dipole[pl.ds(index[c], 1)]
        chosen[c] = jnp.where(orbital == index[c], 1.0, 0.0)
    device = lax.axis_index(("chip", "core", "narrow"))
    rows = lax.broadcasted_iota(jnp.int32, (SUB, LANE), 0)
    tiles = []
    for start in range(0, modes, SUB):
        tile = jnp.zeros((SUB, LANE), F32)
        for k in range(start, start + SUB):
            value = frequency[k % freqs] + energy[index[k // freqs]]
            tile = jnp.where(rows == k - start, value, tile)
        tiles.append(tile)
    shift = jnp.concatenate(tiles, 0)
    for at in range(0, columns, LANE):
        here = jnp.broadcast_to(virt[:, at : at + LANE], (modes, LANE))
        level[:, at : at + LANE] = here - shift
        for s in range(slots):
            offset = pair_shift[blocks[device * slots + s]]
            denom[s, :, at : at + LANE] = (shift - offset) - here
    for (s, r), copy in zip(parts, coupled):
        copy.wait()
        advance(1)
        upper, lower = halves(coupling[s, r])
        high[s, r] = upper
        low[s, r] = lower

def fold(response, slab_t, high, low, dims):
    upper, lower = halves(response)
    both = jnp.concatenate([upper, lower], 0)
    singles = joined(mxu(both, slab_t, INNER))
    doubles = [joined(mxu(both, h, dims)) + mxu(upper, l, dims) for h, l in zip(high, low)]
    return singles, doubles


def quotient(inner, den):
    modes = den.shape[0]
    re, im = inner[:modes], inner[modes:]
    inverse = 1.0 / (den * den + DAMP * DAMP)
    return jnp.concatenate(
        [(re * den + im * DAMP) * inverse, (im * den - re * DAMP) * inverse], 0
    )


def unfold(singles, doubles, amplitudes, high, low, columns):
    total = mxu(singles[...], amplitudes[:, columns], INNER)
    slots, double = doubles.shape[:2]
    for s in range(slots):
        total = total + mxu(doubles[s], high[s, :, columns], INNER)
    total = joined(total)
    for s in range(slots):
        total = total + mxu(doubles[s, : double // 2], low[s, :, columns], INNER)
    return total


def write_tiles(out, total, modes):
    tiles = total.shape[1] // LANE
    for group in range(modes // SUB):
        for tile in range(tiles):
            piece, lanes = group * tiles + tile, slice(tile * LANE, (tile + 1) * LANE)
            out[piece, 0] = total[group * SUB : (group + 1) * SUB, lanes]
            out[piece, 1] = total[modes + group * SUB : modes + (group + 1) * SUB, lanes]


def starting(rhs, level):
    inverse = 1.0 / (level * level + DAMP * DAMP)
    return jnp.concatenate([rhs * level * inverse, rhs * DAMP * inverse], 0)


def first_own_body(own, level, high, low, slab, rhs, start, singles, doubles, slab_t):
    modes, block = rhs.shape
    freqs = modes // own.shape[0]
    here = pl.ds(pl.multiple_of(lax.axis_index("narrow") * block, LANE), block)
    for c in range(own.shape[0]):
        rhs[c * freqs : (c + 1) * freqs] = jnp.broadcast_to(own[c : c + 1], (freqs, block))
    start[...] = starting(rhs[...], level[:, here])
    slots = range(high.shape[0])
    slab_t[...] = slab[...].T
    single, inner = fold(
        start[...],
        slab_t[here],
        [high[s, :, here] for s in slots],
        [low[s, :, here] for s in slots],
        LAST,
    )
    singles[...] = single
    for s, value in enumerate(inner):
        doubles[s] = value


def first_body(
    other,
    chosen,
    level,
    denom,
    high,
    low,
    slab_t,
    rhs_part,
    start_part,
    single_part,
    double_part,
    amplitudes,
    rhs,
    start,
    singles,
    doubles,
    give,
):
    modes, virt = level.shape
    cores, block = chosen.shape[0], other.shape[1]
    freqs = modes // cores
    side = lax.axis_index("narrow")
    here = pl.ds(pl.multiple_of(side * block, LANE), block)
    there = pl.ds(pl.multiple_of((1 - side) * block, LANE), block)
    rhs[:, here] = rhs_part[...]
    start[:, here] = start_part[...]
    for c in range(cores):
        mask = jnp.concatenate([chosen[c]] * (block // LANE), 1)
        theirs = jnp.sum(jnp.where(mask > 0.5, other[...], 0.0), axis=0, keepdims=True)
        rhs[c * freqs : (c + 1) * freqs, there] = jnp.broadcast_to(theirs, (freqs, block))
    rest = starting(rhs[:, there], level[:, there])
    start[:, there] = rest
    slots = range(high.shape[0])
    single, inner = fold(
        rest,
        slab_t[there],
        [high[s, :, there] for s in slots],
        [low[s, :, there] for s in slots],
        LAST,
    )
    singles[...] = stacked(single_part[...] + single)
    for s, value in enumerate(inner):
        doubles[s] = stacked(quotient(double_part[s] + value, denom[s]))
    columns = pl.ds(pl.multiple_of((1 - lax.axis_index("core")) * (virt // 2), LANE), virt // 2)
    write_tiles(give, unfold(singles, doubles, amplitudes, high, low, columns), modes)


def first_rest_body(singles, doubles, amplitudes, high, low, keep, high_t, low_t):
    modes, half = singles.shape[0] // 4, high.shape[2] // 2
    core = lax.axis_index("core")
    columns = pl.ds(pl.multiple_of(core * half, LANE), half)
    rest = pl.ds(pl.multiple_of((1 - core) * half, LANE), half)
    write_tiles(keep, unfold(singles, doubles, amplitudes, high, low, columns), modes)
    for s in range(high.shape[0]):
        high_t[s] = high[s, :, rest].T
        low_t[s] = low[s, :, rest].T


def add_body(left, right, out):
    out[...] = left[...] + right[...]


def first_update_body(got, level, rhs, start, sent):
    members = got.shape[0]
    modes, virt = level.shape
    tiles = virt // 2 // LANE
    mine = lax.axis_index(("chip", "narrow"))
    group, tile = lax.div(mine, tiles), lax.rem(mine, tiles)
    column = lax.axis_index("core") * (virt // 2) + tile * LANE
    columns = pl.ds(pl.multiple_of(column, LANE), LANE)
    rows = pl.ds(pl.multiple_of(group * SUB, SUB), SUB)
    total = got[0]
    for j in range(1, members):
        total = total + got[j]
    lev, right = level[rows, columns], rhs[rows, columns]
    re = start[rows, columns]
    im = start[pl.ds(pl.multiple_of(modes + group * SUB, SUB), SUB), columns]
    inverse = 1.0 / (lev * lev + DAMP * DAMP)
    res_re = right - (lev * re + DAMP * im + total[0])
    res_im = -(lev * im - DAMP * re + total[1])
    re = re + (res_re * lev - res_im * DAMP) * inverse
    im = im + (res_im * lev + res_re * DAMP) * inverse
    for j in range(members):
        sent[j, 0] = re
        sent[j, 1] = im


def read_tiles(part, modes):
    tiles = part.shape[0] // (modes // SUB)
    rows = [
        jnp.concatenate([part[group * tiles + tile, q] for tile in range(tiles)], 1)
        for q in range(2)
        for group in range(modes // SUB)
    ]
    return jnp.concatenate(rows, 0)


def second_own_body(own, slab_t, high, low, response, singles, doubles):
    modes, half = response.shape[0] // 2, response.shape[1]
    mine = pl.ds(pl.multiple_of(lax.axis_index("core") * half, LANE), half)
    slots = range(high.shape[0])
    response[...] = read_tiles(own, modes)
    single, inner = fold(
        response[...],
        slab_t[mine],
        [high[s, :, mine] for s in slots],
        [low[s, :, mine] for s in slots],
        LAST,
    )
    singles[...] = single
    for s, value in enumerate(inner):
        doubles[s] = value


def write_owned(out, singles, doubles, amplitudes, high, low, at):
    members, double, half = out.shape
    owned, quarter = double // 2, half // 2
    modes = members * owned
    for side in range(2):
        columns = pl.ds(pl.multiple_of(side * half + at * quarter, LANE), quarter)
        total = unfold(singles, doubles, amplitudes, high, low, columns)
        lanes = slice(side * quarter, (side + 1) * quarter)
        for j in range(members):
            out[j, :owned, lanes] = total[j * owned : (j + 1) * owned]
            out[j, owned:, lanes] = total[modes + j * owned : modes + (j + 1) * owned]


def second_body(
    mine,
    other,
    single_part,
    double_part,
    denom,
    high,
    low,
    high_t,
    low_t,
    slab_t,
    amplitudes,
    response,
    singles,
    doubles,
    give,
):
    half = mine.shape[1]
    modes = mine.shape[0] // 2
    core = lax.axis_index("core")
    columns = pl.ds(pl.multiple_of(core * half, LANE), half)
    rest = pl.ds(pl.multiple_of((1 - core) * half, LANE), half)
    theirs = read_tiles(other, modes)
    response[:, columns] = mine[...]
    response[:, rest] = theirs
    slots = range(high_t.shape[0])
    single, inner = fold(
        theirs, slab_t[rest], [high_t[s] for s in slots], [low_t[s] for s in slots], INNER
    )
    singles[...] = stacked(single_part[...] + single)
    for s, value in enumerate(inner):
        doubles[s] = stacked(quotient(double_part[s] + value, denom[s]))
    write_owned(give, singles, doubles, amplitudes, high, low, 1 - core)


def second_rest_body(
    singles, doubles, amplitudes, high, low, level, start, response, keep, squares
):
    write_owned(keep, singles, doubles, amplitudes, high, low, lax.axis_index("core"))
    modes = level.shape[0]
    lev = level[...]
    re = response[:modes] - start[:modes]
    im = response[modes:] - start[modes:]
    res_re = lev * re + DAMP * im
    res_im = lev * im - DAMP * re
    squares[...] = jnp.sum(res_re * res_re + res_im * res_im, axis=1, keepdims=True)


def second_update_body(got, level, rhs, response, sent):
    members, double, width = got.shape
    owned = double // 2
    modes, virt = level.shape
    half, quarter = virt // 2, virt // 4
    mine = lax.axis_index(("chip", "narrow"))
    core = lax.axis_index("core")
    total = got[0]
    for j in range(1, members):
        total = total + got[j]
    per_tile = SUB // owned
    within = lax.rem(mine, per_tile)

    def own_rows(ref, first, columns):
        at = first + lax.div(mine, per_tile) * SUB
        tile = ref[pl.ds(pl.multiple_of(at, SUB), SUB), columns]
        rows = tile[:owned]
        for q in range(1, per_tile):
            rows = jnp.where(within == q, tile[q * owned : (q + 1) * owned], rows)
        return rows

    squares = jnp.zeros((owned, 1), F32)
    fresh = []
    for side in range(2):
        columns = pl.ds(pl.multiple_of(side * half + core * quarter, LANE), quarter)
        lanes = slice(side * quarter, (side + 1) * quarter)
        lev, right = own_rows(level, 0, columns), own_rows(rhs, 0, columns)
        re, im = own_rows(response, 0, columns), own_rows(response, modes, columns)
        inverse = 1.0 / (lev * lev + DAMP * DAMP)
        res_re = right - (lev * re + DAMP * im + total[:owned, lanes])
        res_im = -(lev * im - DAMP * re + total[owned:, lanes])
        squares += jnp.sum(res_re * res_re + res_im * res_im, axis=1, keepdims=True)
        re = re + (res_re * lev - res_im * DAMP) * inverse
        im = im + (res_im * lev + res_re * DAMP) * inverse
        fresh.append(jnp.concatenate([re, im], 0))
    lane = lax.broadcasted_iota(jnp.int32, (1, LANE), 1)
    tail = jnp.zeros((1, LANE), F32)
    for i in range(owned):
        tail = jnp.where(lane == i, jnp.broadcast_to(squares[i : i + 1], (1, LANE)), tail)
    for j in range(sent.shape[0]):
        for i in range(double):
            sent[j, :, i * quarter : (i + 1) * quarter] = fresh[j % 2][i : i + 1]
        sent[j, :, double * quarter :] = tail


def finish_body(got, old, response, rms):
    devices = got.shape[0]
    quarter = response.shape[2] // 2
    sweeps, modes = rms.shape
    owned = 2 * modes // devices
    double = 2 * owned
    row = lax.broadcasted_iota(jnp.int32, (sweeps, LANE), 0)
    lane = lax.broadcasted_iota(jnp.int32, (sweeps, LANE), 1)
    squares = jnp.zeros((sweeps, LANE), F32)
    for chip in range(devices // 4):
        for side in range(2):
            sources = [(chip * 2 + core) * 2 + side for core in range(2)]
            first = (chip * 2 + side) * owned
            for core, j in enumerate(sources):
                columns = slice(core * quarter, (core + 1) * quarter)
                for i in range(double):
                    k = first + i % owned
                    response[i // owned, k : k + 1, columns] = got[
                        j, :, i * quarter : (i + 1) * quarter
                    ]
            both = sum(got[j, :, double * quarter :] for j in sources)
            for i in range(owned):
                k = first + i
                value = jnp.broadcast_to(both[:, i : i + 1], (sweeps, LANE))
                squares = jnp.where((row == 1) & (lane == k), value, squares)
                value = jnp.broadcast_to(old[k : k + 1], (sweeps, LANE))
                squares = jnp.where((row == 0) & (lane == k), value, squares)
    virt = 4 * quarter
    rms[...] = jnp.sqrt(squares / (2 * virt) + 1e-6)[:, :modes]


def fast_path(
    chips,
    narrow,
    amplitudes,
    integral_slab,
    coupling,
    pair_of_block,
    pair_shift,
    virt_energy,
    core_energy,
    core_index,
    frequency,
    dipole,
):
    virt = virt_energy.shape[0]
    cores = core_index.shape[0]
    modes = frequency.shape[0] * cores
    slots = coupling.shape[0]
    block = dipole.shape[1]
    rows = amplitudes.shape[0]
    members = chips * narrow
    half = virt // 2
    flip_core = [(0, 1), (1, 0)]
    group = ("chip", "narrow")
    work = 8 * modes * virt * (virt * slots + rows)
    size = 2 * virt * (2 * virt * slots + rows)

    across = lax.ppermute(dipole, "narrow", flip_core)
    scalars = (core_index, core_energy, frequency, pair_of_block, pair_shift)
    picked, chosen, level, denom, high, low = call(
        prepare_body,
        "prepare",
        scalars + (virt_energy[None], dipole, coupling),
        [HBM] * 8,
        [((cores, block), F32), ((cores, dipole.shape[0], LANE), F32)]
        + [((modes, virt), F32), ((slots, modes, virt), F32)]
        + [((slots, virt, virt), BF16)] * 2,
        scratch=[pltpu.SMEM(a.shape, a.dtype) for a in scalars]
        + [
            pltpu.VMEM((1, virt), F32),
            pltpu.VMEM(dipole.shape, F32),
            pltpu.VMEM(coupling.shape, F32),
            pltpu.SemaphoreType.DMA((7,)),
            pltpu.SemaphoreType.DMA((PARTS * slots,)),
        ],
        flops=4 * slots * virt * virt,
        moved=2 * size,
    )
    piece = (members, 2, SUB, LANE)
    between = [((4 * modes, rows), BF16), ((slots, 4 * modes, virt), BF16)]
    *parts, slab_t = call(
        first_own_body,
        "first_own",
        (picked, level, high, low, integral_slab),
        [VMEM] * 5,
        [((modes, block), F32), ((2 * modes, block), F32)]
        + [((2 * modes, rows), F32), ((slots, 2 * modes, virt), F32)]
        + [((virt, rows), BF16)],
        flops=work // 4,
        moved=size // 2,
    )
    rhs, start, singles, doubles, give = call(
        first_body,
        "first",
        (across, chosen, level, denom, high, low, slab_t, *parts, amplitudes),
        [VMEM] * 12,
        [((modes, virt), F32), ((2 * modes, virt), F32)]
        + between
        + [(piece, F32)],
        flops=work * 3 // 4,
        moved=2 * size,
    )
    got = lax.ppermute(give, "core", flip_core)
    keep, high_t, low_t = call(
        first_rest_body,
        "first_rest",
        (singles, doubles, amplitudes, high, low),
        [VMEM] * 5,
        [(piece, F32)] + [((slots, half, virt), BF16)] * 2,
        flops=work // 4,
        moved=size // 2,
    )
    (total,) = call(add_body, "add_first", (keep, got), [VMEM] * 2, [(piece, F32)])
    got = lax.all_to_all(total, group, 0, 0, tiled=True)
    (sent,) = call(
        first_update_body, "first_update", (got, level, rhs, start), [VMEM] * 4, [(piece, F32)]
    )
    got = lax.all_to_all(sent, group, 0, 0, tiled=True)
    other = lax.ppermute(got, "core", flip_core)
    owned = modes // members
    piece = (members, 2 * owned, half)
    mine, single_part, double_part = call(
        second_own_body,
        "second_own",
        (got, slab_t, high, low),
        [VMEM] * 4,
        [
            ((2 * modes, half), F32),
            ((2 * modes, rows), F32),
            ((slots, 2 * modes, virt), F32),
        ],
        flops=work // 4,
        moved=size // 2,
    )
    response, singles, doubles, give = call(
        second_body,
        "second",
        (mine, other, single_part, double_part, denom, high, low, high_t, low_t, slab_t, amplitudes),
        [VMEM] * 11,
        [((2 * modes, virt), F32)] + between + [(piece, F32)],
        flops=work // 2,
        moved=size,
    )
    got = lax.ppermute(give, "core", flip_core)
    keep, old = call(
        second_rest_body,
        "second_rest",
        (singles, doubles, amplitudes, high, low, level, start, response),
        [VMEM] * 8,
        [(piece, F32), ((modes, 1), F32)],
        flops=work // 4,
        moved=size // 2,
    )
    (total,) = call(add_body, "add_second", (keep, got), [VMEM] * 2, [(piece, F32)])
    got = lax.all_to_all(total, group, 0, 0, tiled=True)
    piece = (2 * members, 1, owned * virt // 2 + LANE)
    (sent,) = call(
        second_update_body,
        "second_update",
        (got, level, rhs, response),
        [VMEM] * 4,
        [(piece, F32)],
    )
    got = lax.all_to_all(sent, ("chip", "core", "narrow"), 0, 0, tiled=True)
    return tuple(
        call(
            finish_body,
            "finish",
            (got, old),
            [VMEM] * 2,
            [((2, modes, block), F32), ((ITERS, modes), F32)],
        )
    )


def plain_path(
    wide,
    narrow,
    amplitudes,
    integral_slab,
    coupling,
    pair_of_block,
    pair_shift,
    virt_energy,
    core_energy,
    core_index,
    frequency,
    dipole,
):
    virt = virt_energy.shape[0]
    freqs = frequency.shape[0]
    modes = freqs * core_index.shape[0]
    slots = coupling.shape[0]
    block = dipole.shape[1]
    everyone = modes % (wide * narrow) == 0
    group = ("chip", "core", "narrow") if everyone else ("chip", "core")
    members = wide * narrow if everyone else wide
    owned = modes // members

    here = lax.axis_index(("chip", "core", "narrow"))
    mine = lax.axis_index(group)
    picked = jnp.take(dipole, core_index, axis=0)
    picked = lax.all_gather(picked, "narrow", axis=1, tiled=True)
    shift = (frequency[None, :] + jnp.take(core_energy, core_index)[:, None]).reshape(-1)
    offset = jnp.take(pair_shift, lax.dynamic_slice_in_dim(pair_of_block, here * slots, slots))
    rhs = jnp.repeat(picked, freqs, axis=0)
    level = virt_energy[None, :] - shift[:, None]
    mag = level * level + DAMP * DAMP
    response = jnp.concatenate([rhs * level / mag, rhs * DAMP / mag], 0)
    den = shift[None, :, None] - offset[:, None, None] - virt_energy[None, None, :]
    den_mag = den * den + DAMP * DAMP
    own_rhs = lax.dynamic_slice_in_dim(rhs, mine * owned, owned)
    own_level = lax.dynamic_slice_in_dim(level, mine * owned, owned)
    own_mag = own_level * own_level + DAMP * DAMP
    own_re, own_im = own_rhs * own_level / own_mag, own_rhs * DAMP / own_mag
    slab = integral_slab.astype(F32)
    ampl = amplitudes.astype(F32)

    def dot(left, right, dims):
        return lax.dot_general(left, right, dims, precision=HIGHEST, preferred_element_type=F32)

    rms = []
    for sweep in range(ITERS):
        folded = dot(dot(response, slab, LAST), ampl, INNER)
        for slot in range(slots):
            inner = dot(response, coupling[slot], LAST)
            re, im = inner[:modes], inner[modes:]
            quot = jnp.concatenate(
                [
                    (re * den[slot] + im * DAMP) / den_mag[slot],
                    (im * den[slot] - re * DAMP) / den_mag[slot],
                ],
                0,
            )
            folded = folded + dot(quot, coupling[slot], INNER)
        pieces = folded.reshape(2, members, owned, virt).transpose(1, 0, 2, 3)
        total = jnp.sum(lax.all_to_all(pieces, group, 0, 0, tiled=True), 0)
        if not everyone:
            total = lax.psum(total, "narrow")
        res_re = own_rhs - (own_level * own_re + DAMP * own_im + total[0])
        res_im = -(own_level * own_im - DAMP * own_re + total[1])
        squares = jnp.sum(res_re * res_re + res_im * res_im, axis=1)
        rms.append(jnp.sqrt(squares / (2 * virt) + 1e-6))
        own_re = own_re + (res_re * own_level - res_im * DAMP) / own_mag
        own_im = own_im + (res_im * own_level + res_re * DAMP) / own_mag
        own = jnp.stack([own_re, own_im], 0)
        if sweep + 1 < ITERS:
            sent = jnp.broadcast_to(own[None], (members,) + own.shape)
            got = lax.all_to_all(sent, group, 0, 0, tiled=True)
            response = got.transpose(1, 0, 2, 3).reshape(2 * modes, virt)
    if everyone:
        sent = own.reshape(2, owned, narrow, block).transpose(2, 0, 1, 3)
        sent = jnp.broadcast_to(sent[None], (wide,) + sent.shape).reshape(members, 2, owned, block)
    else:
        sent = lax.dynamic_slice_in_dim(own, lax.axis_index("narrow") * block, block, 2)
        sent = jnp.broadcast_to(sent[None], (members,) + sent.shape)
    extra = jnp.broadcast_to(jnp.stack(rms, 0)[None, :, :, None], (members, 2, owned, LANE))
    got = lax.all_to_all(jnp.concatenate([sent, extra], 3), group, 0, 0, tiled=True)
    got = got.transpose(1, 0, 2, 3).reshape(2, modes, block + LANE)
    return got[:, :, :block], got[:, :, block]


def solution(mesh):
    wide, narrow = mesh.shape["wide"], mesh.shape["narrow"]
    chips = wide // 2
    finer = Mesh(mesh.devices.reshape(chips, 2, narrow), ("chip", "core", "narrow"))
    split = ("chip", "core", "narrow")

    def body(*args):
        virt, modes = args[5].shape[0], args[8].shape[0] * args[7].shape[0]
        pieces = (modes // SUB) * (virt // LANE)
        fits = (
            narrow == 2
            and pieces == 2 * chips * narrow
            and modes % (chips * narrow) == 0
            and SUB % (modes // (chips * narrow)) == 0
            and virt % (4 * LANE) == 0
        )
        if fits:
            return fast_path(chips, narrow, *args)
        return plain_path(wide, narrow, *args)

    return jax.shard_map(
        body,
        mesh=finer,
        in_specs=(
            P(split, None),
            P(split, None),
            P(split, None, None),
            P(),
            P(),
            P(),
            P(),
            P(),
            P(),
            P(None, "narrow"),
        ),
        out_specs=(P(None, None, "narrow"), P()),
        check_vma=False,
    )
```

```python
from functools import partial

import jax
import jax.numpy as jnp
from jax import lax
from jax.experimental import pallas as pl
from jax.experimental.pallas import tpu as pltpu
from jax.sharding import Mesh, PartitionSpec as P

ITERS = 2
DAMP = 0.5
HIGHEST = lax.Precision.HIGHEST
F32, BF16 = jnp.float32, jnp.bfloat16
LAST = (((1,), (1,)), ((), ()))
INNER = (((1,), (0,)), ((), ()))
SUB, LANE = 8, 128
VMEM = pl.BlockSpec(memory_space=pltpu.VMEM)
SMEM = pl.BlockSpec(memory_space=pltpu.SMEM)
HBM = pl.BlockSpec(memory_space=pltpu.HBM)
PARTS = 4
WINDOW = 6


def mxu(left, right, dims):
    return lax.dot_general(left, right, dims, preferred_element_type=F32)


def halves(value):
    high = value.astype(BF16)
    return high, (value - high.astype(F32)).astype(BF16)


def stacked(value):
    return jnp.concatenate(halves(value), 0)


def joined(value):
    rows = value.shape[0] // 2
    return value[:rows] + value[rows:]


def call(body, name, operands, in_specs, outs, scratch=(), flops=0, moved=0, aliases={}):
    operands = [
        pltpu.with_memory_space_constraint(x, pltpu.HBM) if spec is HBM else x
        for x, spec in zip(operands, in_specs)
    ]
    return pl.pallas_call(
        body,
        out_shape=[jax.ShapeDtypeStruct(s, d) for s, d in outs],
        in_specs=in_specs,
        out_specs=[VMEM] * len(outs),
        scratch_shapes=scratch,
        name=name,
        input_output_aliases=aliases,
        compiler_params=pltpu.CompilerParams(vmem_limit_bytes=20 << 20),
        cost_estimate=pl.CostEstimate(flops=flops, bytes_accessed=moved, transcendentals=0),
    )(*operands)


def start_all(pairs, sems):
    copies = [pltpu.make_async_copy(src, dst, sems.at[i]) for i, (src, dst) in enumerate(pairs)]
    for copy in copies:
        copy.start()
    return copies


def prepare_body(
    index_hbm,
    energy_hbm,
    frequency_hbm,
    blocks_hbm,
    pair_shift_hbm,
    virt_hbm,
    dipole_hbm,
    coupling_hbm,
    picked,
    chosen,
    level,
    denom,
    high,
    low,
    index,
    energy,
    frequency,
    blocks,
    pair_shift,
    virt,
    dipole,
    coupling,
    small_sems,
    coupling_sems,
):
    freqs = frequency.shape[0]
    modes, columns = level.shape
    slots = coupling.shape[0]
    small = start_all(
        [
            (index_hbm, index),
            (energy_hbm, energy),
            (frequency_hbm, frequency),
            (blocks_hbm, blocks),
            (pair_shift_hbm, pair_shift),
            (virt_hbm, virt),
            (dipole_hbm, dipole),
        ],
        small_sems,
    )
    step = coupling.shape[1] // PARTS
    parts = [(s, slice(i * step, (i + 1) * step)) for s in range(slots) for i in range(PARTS)]
    coupled = [
        pltpu.make_async_copy(coupling_hbm.at[s, r], coupling.at[s, r], coupling_sems.at[i])
        for i, (s, r) in enumerate(parts)
    ]
    waiting = list(coupled)

    def advance(count):
        for copy in waiting[:count]:
            copy.start()
        del waiting[:count]

    advance(WINDOW)
    for copy in small:
        copy.wait()
    orbital = lax.broadcasted_iota(jnp.int32, chosen.shape[1:], 0)
    for c in range(index.shape[0]):
        picked[c : c + 1] = dipole[pl.ds(index[c], 1)]
        chosen[c] = jnp.where(orbital == index[c], 1.0, 0.0)
    device = lax.axis_index(("chip", "core", "narrow"))
    rows = lax.broadcasted_iota(jnp.int32, (SUB, LANE), 0)
    tiles = []
    for start in range(0, modes, SUB):
        tile = jnp.zeros((SUB, LANE), F32)
        for k in range(start, start + SUB):
            value = frequency[k % freqs] + energy[index[k // freqs]]
            tile = jnp.where(rows == k - start, value, tile)
        tiles.append(tile)
    shift = jnp.concatenate(tiles, 0)
    for at in range(0, columns, LANE):
        here = jnp.broadcast_to(virt[:, at : at + LANE], (modes, LANE))
        level[:, at : at + LANE] = here - shift
        for s in range(slots):
            offset = pair_shift[blocks[device * slots + s]]
            denom[s, :, at : at + LANE] = (shift - offset) - here
    for (s, r), copy in zip(parts, coupled):
        copy.wait()
        advance(1)
        upper, lower = halves(coupling[s, r])
        high[s, r] = upper
        low[s, r] = lower

def fold(response, slab_t, high, low, dims):
    upper, lower = halves(response)
    both = jnp.concatenate([upper, lower], 0)
    singles = joined(mxu(both, slab_t, INNER))
    doubles = [joined(mxu(both, h, dims)) + mxu(upper, l, dims) for h, l in zip(high, low)]
    return singles, doubles


def quotient(inner, den):
    modes = den.shape[0]
    re, im = inner[:modes], inner[modes:]
    inverse = 1.0 / (den * den + DAMP * DAMP)
    return jnp.concatenate(
        [(re * den + im * DAMP) * inverse, (im * den - re * DAMP) * inverse], 0
    )


def unfold(singles, doubles, amplitudes, high, low, columns):
    total = mxu(singles[...], amplitudes[:, columns], INNER)
    slots, double = doubles.shape[:2]
    for s in range(slots):
        total = total + mxu(doubles[s], high[s, :, columns], INNER)
    total = joined(total)
    for s in range(slots):
        total = total + mxu(doubles[s, : double // 2], low[s, :, columns], INNER)
    return total


def write_tiles(out, total, modes):
    tiles = total.shape[1] // LANE
    for group in range(modes // SUB):
        for tile in range(tiles):
            piece, lanes = group * tiles + tile, slice(tile * LANE, (tile + 1) * LANE)
            out[piece, 0] = total[group * SUB : (group + 1) * SUB, lanes]
            out[piece, 1] = total[modes + group * SUB : modes + (group + 1) * SUB, lanes]


def starting(rhs, level):
    inverse = 1.0 / (level * level + DAMP * DAMP)
    return jnp.concatenate([rhs * level * inverse, rhs * DAMP * inverse], 0)


def first_own_body(own, level, high, low, slab, rhs, start, singles, doubles, slab_t):
    modes, block = rhs.shape
    freqs = modes // own.shape[0]
    here = pl.ds(pl.multiple_of(lax.axis_index("narrow") * block, LANE), block)
    for c in range(own.shape[0]):
        rhs[c * freqs : (c + 1) * freqs] = jnp.broadcast_to(own[c : c + 1], (freqs, block))
    start[...] = starting(rhs[...], level[:, here])
    slots = range(high.shape[0])
    slab_t[here] = slab[:, here].T
    single, inner = fold(
        start[...],
        slab_t[here],
        [high[s, :, here] for s in slots],
        [low[s, :, here] for s in slots],
        LAST,
    )
    singles[...] = single
    for s, value in enumerate(inner):
        doubles[s] = value


def first_body(
    other,
    chosen,
    level,
    denom,
    high,
    low,
    _,
    slab,
    rhs_part,
    start_part,
    single_part,
    double_part,
    amplitudes,
    rhs,
    start,
    singles,
    doubles,
    give,
    slab_t,
):
    modes, virt = level.shape
    cores, block = chosen.shape[0], other.shape[1]
    freqs = modes // cores
    side = lax.axis_index("narrow")
    here = pl.ds(pl.multiple_of(side * block, LANE), block)
    there = pl.ds(pl.multiple_of((1 - side) * block, LANE), block)
    rhs[:, here] = rhs_part[...]
    start[:, here] = start_part[...]
    for c in range(cores):
        mask = jnp.concatenate([chosen[c]] * (block // LANE), 1)
        theirs = jnp.sum(jnp.where(mask > 0.5, other[...], 0.0), axis=0, keepdims=True)
        rhs[c * freqs : (c + 1) * freqs, there] = jnp.broadcast_to(theirs, (freqs, block))
    rest = starting(rhs[:, there], level[:, there])
    start[:, there] = rest
    slab_t[there] = slab[:, there].T
    slots = range(high.shape[0])
    single, inner = fold(
        rest,
        slab_t[there],
        [high[s, :, there] for s in slots],
        [low[s, :, there] for s in slots],
        LAST,
    )
    singles[...] = stacked(single_part[...] + single)
    for s, value in enumerate(inner):
        doubles[s] = stacked(quotient(double_part[s] + value, denom[s]))
    columns = pl.ds(pl.multiple_of((1 - lax.axis_index("core")) * (virt // 2), LANE), virt // 2)
    write_tiles(give, unfold(singles, doubles, amplitudes, high, low, columns), modes)


def first_rest_body(singles, doubles, amplitudes, high, low, keep, high_t, low_t):
    modes, half = singles.shape[0] // 4, high.shape[2] // 2
    core = lax.axis_index("core")
    columns = pl.ds(pl.multiple_of(core * half, LANE), half)
    rest = pl.ds(pl.multiple_of((1 - core) * half, LANE), half)
    write_tiles(keep, unfold(singles, doubles, amplitudes, high, low, columns), modes)
    for s in range(high.shape[0]):
        high_t[s] = high[s, :, rest].T
        low_t[s] = low[s, :, rest].T


def add_body(left, right, out):
    out[...] = left[...] + right[...]


def first_update_body(got, level, rhs, start, sent):
    members = got.shape[0]
    modes, virt = level.shape
    tiles = virt // 2 // LANE
    mine = lax.axis_index(("chip", "narrow"))
    group, tile = lax.div(mine, tiles), lax.rem(mine, tiles)
    column = lax.axis_index("core") * (virt // 2) + tile * LANE
    columns = pl.ds(pl.multiple_of(column, LANE), LANE)
    rows = pl.ds(pl.multiple_of(group * SUB, SUB), SUB)
    total = got[0]
    for j in range(1, members):
        total = total + got[j]
    lev, right = level[rows, columns], rhs[rows, columns]
    re = start[rows, columns]
    im = start[pl.ds(pl.multiple_of(modes + group * SUB, SUB), SUB), columns]
    inverse = 1.0 / (lev * lev + DAMP * DAMP)
    res_re = right - (lev * re + DAMP * im + total[0])
    res_im = -(lev * im - DAMP * re + total[1])
    re = re + (res_re * lev - res_im * DAMP) * inverse
    im = im + (res_im * lev + res_re * DAMP) * inverse
    for j in range(members):
        sent[j, 0] = re
        sent[j, 1] = im


def read_tiles(part, modes):
    tiles = part.shape[0] // (modes // SUB)
    rows = [
        jnp.concatenate([part[group * tiles + tile, q] for tile in range(tiles)], 1)
        for q in range(2)
        for group in range(modes // SUB)
    ]
    return jnp.concatenate(rows, 0)


def second_own_body(own, slab_t, high, low, response, singles, doubles):
    modes, half = response.shape[0] // 2, response.shape[1]
    mine = pl.ds(pl.multiple_of(lax.axis_index("core") * half, LANE), half)
    slots = range(high.shape[0])
    response[...] = read_tiles(own, modes)
    single, inner = fold(
        response[...],
        slab_t[mine],
        [high[s, :, mine] for s in slots],
        [low[s, :, mine] for s in slots],
        LAST,
    )
    singles[...] = single
    for s, value in enumerate(inner):
        doubles[s] = value


def write_owned(out, singles, doubles, amplitudes, high, low, at):
    members, double, half = out.shape
    owned, quarter = double // 2, half // 2
    modes = members * owned
    for side in range(2):
        columns = pl.ds(pl.multiple_of(side * half + at * quarter, LANE), quarter)
        total = unfold(singles, doubles, amplitudes, high, low, columns)
        lanes = slice(side * quarter, (side + 1) * quarter)
        for j in range(members):
            out[j, :owned, lanes] = total[j * owned : (j + 1) * owned]
            out[j, owned:, lanes] = total[modes + j * owned : modes + (j + 1) * owned]


def second_body(
    mine,
    other,
    single_part,
    double_part,
    denom,
    high,
    low,
    high_t,
    low_t,
    slab_t,
    amplitudes,
    response,
    singles,
    doubles,
    give,
):
    half = mine.shape[1]
    modes = mine.shape[0] // 2
    core = lax.axis_index("core")
    columns = pl.ds(pl.multiple_of(core * half, LANE), half)
    rest = pl.ds(pl.multiple_of((1 - core) * half, LANE), half)
    theirs = read_tiles(other, modes)
    response[:, columns] = mine[...]
    response[:, rest] = theirs
    slots = range(high_t.shape[0])
    single, inner = fold(
        theirs, slab_t[rest], [high_t[s] for s in slots], [low_t[s] for s in slots], INNER
    )
    singles[...] = stacked(single_part[...] + single)
    for s, value in enumerate(inner):
        doubles[s] = stacked(quotient(double_part[s] + value, denom[s]))
    write_owned(give, singles, doubles, amplitudes, high, low, 1 - core)


def second_rest_body(
    singles, doubles, amplitudes, high, low, level, start, response, keep, squares
):
    write_owned(keep, singles, doubles, amplitudes, high, low, lax.axis_index("core"))
    modes = level.shape[0]
    lev = level[...]
    re = response[:modes] - start[:modes]
    im = response[modes:] - start[modes:]
    res_re = lev * re + DAMP * im
    res_im = lev * im - DAMP * re
    squares[...] = jnp.sum(res_re * res_re + res_im * res_im, axis=1, keepdims=True)


def second_update_body(got, level, rhs, response, sent):
    members, double, width = got.shape
    owned = double // 2
    modes, virt = level.shape
    half, quarter = virt // 2, virt // 4
    mine = lax.axis_index(("chip", "narrow"))
    core = lax.axis_index("core")
    total = got[0]
    for j in range(1, members):
        total = total + got[j]
    per_tile = SUB // owned
    within = lax.rem(mine, per_tile)

    def own_rows(ref, first, columns):
        at = first + lax.div(mine, per_tile) * SUB
        tile = ref[pl.ds(pl.multiple_of(at, SUB), SUB), columns]
        rows = tile[:owned]
        for q in range(1, per_tile):
            rows = jnp.where(within == q, tile[q * owned : (q + 1) * owned], rows)
        return rows

    squares = jnp.zeros((owned, 1), F32)
    fresh = []
    for side in range(2):
        columns = pl.ds(pl.multiple_of(side * half + core * quarter, LANE), quarter)
        lanes = slice(side * quarter, (side + 1) * quarter)
        lev, right = own_rows(level, 0, columns), own_rows(rhs, 0, columns)
        re, im = own_rows(response, 0, columns), own_rows(response, modes, columns)
        inverse = 1.0 / (lev * lev + DAMP * DAMP)
        res_re = right - (lev * re + DAMP * im + total[:owned, lanes])
        res_im = -(lev * im - DAMP * re + total[owned:, lanes])
        squares += jnp.sum(res_re * res_re + res_im * res_im, axis=1, keepdims=True)
        re = re + (res_re * lev - res_im * DAMP) * inverse
        im = im + (res_im * lev + res_re * DAMP) * inverse
        fresh.append(jnp.concatenate([re, im], 0))
    lane = lax.broadcasted_iota(jnp.int32, (1, LANE), 1)
    tail = jnp.zeros((1, LANE), F32)
    for i in range(owned):
        tail = jnp.where(lane == i, jnp.broadcast_to(squares[i : i + 1], (1, LANE)), tail)
    for j in range(sent.shape[0]):
        for i in range(double):
            sent[j, :, i * quarter : (i + 1) * quarter] = fresh[j % 2][i : i + 1]
        sent[j, :, double * quarter :] = tail


def finish_body(got, old, response, rms):
    devices = got.shape[0]
    quarter = response.shape[2] // 2
    sweeps, modes = rms.shape
    owned = 2 * modes // devices
    double = 2 * owned
    row = lax.broadcasted_iota(jnp.int32, (sweeps, LANE), 0)
    lane = lax.broadcasted_iota(jnp.int32, (sweeps, LANE), 1)
    squares = jnp.zeros((sweeps, LANE), F32)
    for chip in range(devices // 4):
        for side in range(2):
            sources = [(chip * 2 + core) * 2 + side for core in range(2)]
            first = (chip * 2 + side) * owned
            for core, j in enumerate(sources):
                columns = slice(core * quarter, (core + 1) * quarter)
                for i in range(double):
                    k = first + i % owned
                    response[i // owned, k : k + 1, columns] = got[
                        j, :, i * quarter : (i + 1) * quarter
                    ]
            both = sum(got[j, :, double * quarter :] for j in sources)
            for i in range(owned):
                k = first + i
                value = jnp.broadcast_to(both[:, i : i + 1], (sweeps, LANE))
                squares = jnp.where((row == 1) & (lane == k), value, squares)
                value = jnp.broadcast_to(old[k : k + 1], (sweeps, LANE))
                squares = jnp.where((row == 0) & (lane == k), value, squares)
    virt = 4 * quarter
    rms[...] = jnp.sqrt(squares / (2 * virt) + 1e-6)[:, :modes]


def fast_path(
    chips,
    narrow,
    amplitudes,
    integral_slab,
    coupling,
    pair_of_block,
    pair_shift,
    virt_energy,
    core_energy,
    core_index,
    frequency,
    dipole,
):
    virt = virt_energy.shape[0]
    cores = core_index.shape[0]
    modes = frequency.shape[0] * cores
    slots = coupling.shape[0]
    block = dipole.shape[1]
    rows = amplitudes.shape[0]
    members = chips * narrow
    half = virt // 2
    flip_core = [(0, 1), (1, 0)]
    group = ("chip", "narrow")
    work = 8 * modes * virt * (virt * slots + rows)
    size = 2 * virt * (2 * virt * slots + rows)

    across = lax.ppermute(dipole, "narrow", flip_core)
    scalars = (core_index, core_energy, frequency, pair_of_block, pair_shift)
    picked, chosen, level, denom, high, low = call(
        prepare_body,
        "prepare",
        scalars + (virt_energy[None], dipole, coupling),
        [HBM] * 8,
        [((cores, block), F32), ((cores, dipole.shape[0], LANE), F32)]
        + [((modes, virt), F32), ((slots, modes, virt), F32)]
        + [((slots, virt, virt), BF16)] * 2,
        scratch=[pltpu.SMEM(a.shape, a.dtype) for a in scalars]
        + [
            pltpu.VMEM((1, virt), F32),
            pltpu.VMEM(dipole.shape, F32),
            pltpu.VMEM(coupling.shape, F32),
            pltpu.SemaphoreType.DMA((7,)),
            pltpu.SemaphoreType.DMA((PARTS * slots,)),
        ],
        flops=4 * slots * virt * virt,
        moved=2 * size,
    )
    piece = (members, 2, SUB, LANE)
    between = [((4 * modes, rows), BF16), ((slots, 4 * modes, virt), BF16)]
    *parts, slab_t = call(
        first_own_body,
        "first_own",
        (picked, level, high, low, integral_slab),
        [VMEM] * 5,
        [((modes, block), F32), ((2 * modes, block), F32)]
        + [((2 * modes, rows), F32), ((slots, 2 * modes, virt), F32)]
        + [((virt, rows), BF16)],
        flops=work // 4,
        moved=size // 2,
    )
    rhs, start, singles, doubles, give, slab_t = call(
        first_body,
        "first",
        (across, chosen, level, denom, high, low, slab_t, integral_slab, *parts, amplitudes),
        [VMEM] * 13,
        [((modes, virt), F32), ((2 * modes, virt), F32)]
        + between
        + [(piece, F32), ((virt, rows), BF16)],
        aliases={6: 5},
        flops=work * 3 // 4,
        moved=2 * size,
    )
    got = lax.ppermute(give, "core", flip_core)
    keep, high_t, low_t = call(
        first_rest_body,
        "first_rest",
        (singles, doubles, amplitudes, high, low),
        [VMEM] * 5,
        [(piece, F32)] + [((slots, half, virt), BF16)] * 2,
        flops=work // 4,
        moved=size // 2,
    )
    (total,) = call(add_body, "add_first", (keep, got), [VMEM] * 2, [(piece, F32)])
    got = lax.all_to_all(total, group, 0, 0, tiled=True)
    (sent,) = call(
        first_update_body, "first_update", (got, level, rhs, start), [VMEM] * 4, [(piece, F32)]
    )
    got = lax.all_to_all(sent, group, 0, 0, tiled=True)
    other = lax.ppermute(got, "core", flip_core)
    owned = modes // members
    piece = (members, 2 * owned, half)
    mine, single_part, double_part = call(
        second_own_body,
        "second_own",
        (got, slab_t, high, low),
        [VMEM] * 4,
        [
            ((2 * modes, half), F32),
            ((2 * modes, rows), F32),
            ((slots, 2 * modes, virt), F32),
        ],
        flops=work // 4,
        moved=size // 2,
    )
    response, singles, doubles, give = call(
        second_body,
        "second",
        (mine, other, single_part, double_part, denom, high, low, high_t, low_t, slab_t, amplitudes),
        [VMEM] * 11,
        [((2 * modes, virt), F32)] + between + [(piece, F32)],
        flops=work // 2,
        moved=size,
    )
    got = lax.ppermute(give, "core", flip_core)
    keep, old = call(
        second_rest_body,
        "second_rest",
        (singles, doubles, amplitudes, high, low, level, start, response),
        [VMEM] * 8,
        [(piece, F32), ((modes, 1), F32)],
        flops=work // 4,
        moved=size // 2,
    )
    (total,) = call(add_body, "add_second", (keep, got), [VMEM] * 2, [(piece, F32)])
    got = lax.all_to_all(total, group, 0, 0, tiled=True)
    piece = (2 * members, 1, owned * virt // 2 + LANE)
    (sent,) = call(
        second_update_body,
        "second_update",
        (got, level, rhs, response),
        [VMEM] * 4,
        [(piece, F32)],
    )
    got = lax.all_to_all(sent, ("chip", "core", "narrow"), 0, 0, tiled=True)
    return tuple(
        call(
            finish_body,
            "finish",
            (got, old),
            [VMEM] * 2,
            [((2, modes, block), F32), ((ITERS, modes), F32)],
        )
    )


def plain_path(
    wide,
    narrow,
    amplitudes,
    integral_slab,
    coupling,
    pair_of_block,
    pair_shift,
    virt_energy,
    core_energy,
    core_index,
    frequency,
    dipole,
):
    virt = virt_energy.shape[0]
    freqs = frequency.shape[0]
    modes = freqs * core_index.shape[0]
    slots = coupling.shape[0]
    block = dipole.shape[1]
    everyone = modes % (wide * narrow) == 0
    group = ("chip", "core", "narrow") if everyone else ("chip", "core")
    members = wide * narrow if everyone else wide
    owned = modes // members

    here = lax.axis_index(("chip", "core", "narrow"))
    mine = lax.axis_index(group)
    picked = jnp.take(dipole, core_index, axis=0)
    picked = lax.all_gather(picked, "narrow", axis=1, tiled=True)
    shift = (frequency[None, :] + jnp.take(core_energy, core_index)[:, None]).reshape(-1)
    offset = jnp.take(pair_shift, lax.dynamic_slice_in_dim(pair_of_block, here * slots, slots))
    rhs = jnp.repeat(picked, freqs, axis=0)
    level = virt_energy[None, :] - shift[:, None]
    mag = level * level + DAMP * DAMP
    response = jnp.concatenate([rhs * level / mag, rhs * DAMP / mag], 0)
    den = shift[None, :, None] - offset[:, None, None] - virt_energy[None, None, :]
    den_mag = den * den + DAMP * DAMP
    own_rhs = lax.dynamic_slice_in_dim(rhs, mine * owned, owned)
    own_level = lax.dynamic_slice_in_dim(level, mine * owned, owned)
    own_mag = own_level * own_level + DAMP * DAMP
    own_re, own_im = own_rhs * own_level / own_mag, own_rhs * DAMP / own_mag
    slab = integral_slab.astype(F32)
    ampl = amplitudes.astype(F32)

    def dot(left, right, dims):
        return lax.dot_general(left, right, dims, precision=HIGHEST, preferred_element_type=F32)

    rms = []
    for sweep in range(ITERS):
        folded = dot(dot(response, slab, LAST), ampl, INNER)
        for slot in range(slots):
            inner = dot(response, coupling[slot], LAST)
            re, im = inner[:modes], inner[modes:]
            quot = jnp.concatenate(
                [
                    (re * den[slot] + im * DAMP) / den_mag[slot],
                    (im * den[slot] - re * DAMP) / den_mag[slot],
                ],
                0,
            )
            folded = folded + dot(quot, coupling[slot], INNER)
        pieces = folded.reshape(2, members, owned, virt).transpose(1, 0, 2, 3)
        total = jnp.sum(lax.all_to_all(pieces, group, 0, 0, tiled=True), 0)
        if not everyone:
            total = lax.psum(total, "narrow")
        res_re = own_rhs - (own_level * own_re + DAMP * own_im + total[0])
        res_im = -(own_level * own_im - DAMP * own_re + total[1])
        squares = jnp.sum(res_re * res_re + res_im * res_im, axis=1)
        rms.append(jnp.sqrt(squares / (2 * virt) + 1e-6))
        own_re = own_re + (res_re * own_level - res_im * DAMP) / own_mag
        own_im = own_im + (res_im * own_level + res_re * DAMP) / own_mag
        own = jnp.stack([own_re, own_im], 0)
        if sweep + 1 < ITERS:
            sent = jnp.broadcast_to(own[None], (members,) + own.shape)
            got = lax.all_to_all(sent, group, 0, 0, tiled=True)
            response = got.transpose(1, 0, 2, 3).reshape(2 * modes, virt)
    if everyone:
        sent = own.reshape(2, owned, narrow, block).transpose(2, 0, 1, 3)
        sent = jnp.broadcast_to(sent[None], (wide,) + sent.shape).reshape(members, 2, owned, block)
    else:
        sent = lax.dynamic_slice_in_dim(own, lax.axis_index("narrow") * block, block, 2)
        sent = jnp.broadcast_to(sent[None], (members,) + sent.shape)
    extra = jnp.broadcast_to(jnp.stack(rms, 0)[None, :, :, None], (members, 2, owned, LANE))
    got = lax.all_to_all(jnp.concatenate([sent, extra], 3), group, 0, 0, tiled=True)
    got = got.transpose(1, 0, 2, 3).reshape(2, modes, block + LANE)
    return got[:, :, :block], got[:, :, block]


def solution(mesh):
    wide, narrow = mesh.shape["wide"], mesh.shape["narrow"]
    chips = wide // 2
    finer = Mesh(mesh.devices.reshape(chips, 2, narrow), ("chip", "core", "narrow"))
    split = ("chip", "core", "narrow")

    def body(*args):
        virt, modes = args[5].shape[0], args[8].shape[0] * args[7].shape[0]
        pieces = (modes // SUB) * (virt // LANE)
        fits = (
            narrow == 2
            and pieces == 2 * chips * narrow
            and modes % (chips * narrow) == 0
            and SUB % (modes // (chips * narrow)) == 0
            and virt % (4 * LANE) == 0
        )
        if fits:
            return fast_path(chips, narrow, *args)
        return plain_path(wide, narrow, *args)

    return jax.shard_map(
        body,
        mesh=finer,
        in_specs=(
            P(split, None),
            P(split, None),
            P(split, None, None),
            P(),
            P(),
            P(),
            P(),
            P(),
            P(),
            P(None, "narrow"),
        ),
        out_specs=(P(None, None, "narrow"), P()),
        check_vma=False,
    )
```
